256 devices in a mesh: srow: 32 (over y, x, core), scol: 8 (over z).
Axes of the slice: x: 4, y: 4, z: 8, core: 2. Of those that a mesh axis runs over, the one named last changes fastest.
Arguments:
- factor_state: float32 [32, 512, 4, 8, 512], P('srow', None, None, 'scol'), may hold values from -40 to 40, as said below
- data: float32 [32, 512, 8192], P('srow', None, 'scol'), may hold values from -6 to 6
Outputs:
- factor_out: float32 [32, 512, 4, 8, 512], P('srow', None, None, 'scol')
- data_out: float32 [32, 512, 8192], P('srow', None, 'scol')
The draws below stay inside these ranges and needn't reach their ends.
Inputs may be any that keep to these rules, and one draw needn't show every extreme that they name: factor_state is exactly symmetric and positive definite as the matrix A.
All inputs are finite; a program needn't handle non-finite values.
Results may differ from the reference program's by a relative error of at most 0.00005.
Values sent between devices are 32-bit elements; how exact they have to be, the bound alone decides.
A program may use at most 128 MiB of HBM per device.

```python
import jax
import jax.numpy as jnp
from jax import lax

B = 512
TILES = 32
CYCLE = 8
GROUPS = 4
TIME = 8192


def draw_factor_state(key, part):
    site_count = TILES * B
    latent_rank = 2 * B
    key_latent = jax.random.fold_in(key, 11)
    key_nugget = jax.random.fold_in(key, 12)
    latent = jax.random.normal(key_latent, (site_count, latent_rank), jnp.float32)
    gram_matrix = jnp.dot(latent, latent.T, precision=lax.Precision.HIGHEST) / latent_rank
    nugget = jax.random.uniform(key_nugget, (site_count,), jnp.float32, 0.3, 1.0)
    whole_matrix = gram_matrix + jnp.diag(nugget)
    whole_matrix = 0.5 * (whole_matrix + whole_matrix.T)
    return whole_matrix.reshape(TILES, B, GROUPS, CYCLE, B)


def shard_levels(stream_key, shape, shards, smallest, top_value):
    def one(axis_at, blocks):
        steps = jax.random.uniform(jax.random.fold_in(jax.random.fold_in(stream_key, 6), axis_at), (blocks,), jnp.float32, smallest / len(shards), top_value / len(shards))
        return jnp.repeat(jnp.exp(steps), shape[axis_at] // blocks).reshape((-1,) + (1,) * (len(shape) - axis_at - 1))

    loudness = one(*shards[0])
    for cut in shards[1:]:
        loudness = loudness * one(*cut)
    return loudness


def normal_values(key, dims, width, most, pieces=(), kind=jnp.bfloat16):
    loudness = shard_levels(key, dims, pieces, -0.22, 0.18) if pieces else 1.0
    array = jax.random.normal(key, dims, jnp.float32) * width * loudness
    return jnp.minimum(jnp.maximum(array, -most), most).astype(kind)


def setup_inputs(seed: int = 0) -> dict:
    streams_of = jax.random.split(jax.random.key(seed), 3)
    factor_state = draw_factor_state(jax.random.fold_in(streams_of[2], 71), 0)
    data = normal_values(streams_of[1], (TILES, B, TIME), 1.0, 6.0, ((0, 32), (2, 8)), jnp.float32)
    return {"factor_state": factor_state, "data": data}


def reference(factor_state, data):
    site_count = TILES * B
    highest = lax.Precision.HIGHEST
    whole_matrix = factor_state.reshape(site_count, site_count)
    lower_tile = jnp.linalg.cholesky(whole_matrix[:B, :B])
    panel_tiles = jax.scipy.linalg.solve_triangular(lower_tile, whole_matrix[B:, :B].T, lower=True).T
    trailing = whole_matrix[B:, B:] - jnp.dot(panel_tiles, panel_tiles.T, precision=highest)
    first_rows = jnp.concatenate([lower_tile, jnp.zeros((B, site_count - B), jnp.float32)], axis=1)
    later_rows = jnp.concatenate([panel_tiles, trailing], axis=1)
    factor_out = jnp.concatenate([first_rows, later_rows], axis=0).reshape(TILES, B, GROUPS, CYCLE, B)
    data_matrix = data.reshape(site_count, TIME)
    solved = jax.scipy.linalg.solve_triangular(lower_tile, data_matrix[:B], lower=True)
    remain = data_matrix[B:] - jnp.dot(panel_tiles, solved, precision=highest)
    data_out = jnp.concatenate([solved, remain], axis=0).reshape(TILES, B, TIME)
    return (factor_out, data_out)
```

```python
import functools

import jax
import jax.numpy as jnp
from jax import lax
from jax.experimental import pallas as pl
from jax.experimental.pallas import tpu as pltpu
from jax.sharding import PartitionSpec as P

F32 = jnp.float32
BF16 = jnp.bfloat16
HIGHEST = lax.Precision.HIGHEST
MESH = pl.DeviceIdType.MESH
STEPS = ((1, 0), (0, 1), (-1, 0), (0, -1))
DEPTH = (0, 1, 2, 3, 3, 2, 3, 4, 4, 3, 4, 5, 3, 2, 3, 4)
KIDS = ((0, 1, 2, 5, 6, 10, 14), (1, 5), (5, 9, 13), (1, 2, 14))
HOP = 4
CHUNKS = 24


def tdot(a, b):
    return lax.dot_general(a, b, (((0,), (0,)), ((), ())), precision=HIGHEST, preferred_element_type=F32)


def factor_block(s_ref, u_ref):
    sub = lax.broadcasted_iota(jnp.int32, (8, 128), 0)
    row = s_ref[0:8, :]
    before = None
    for k in range(16):
        lo = 8 * k
        last = k == 15
        if before is not None and not last:
            s_ref[lo + 8 : 128, :] = s_ref[lo + 8 : 128, :] - tdot(before[:, lo + 8 : 128], before)
        c = [jnp.broadcast_to(row[:, lo + m : lo + m + 1], (8, 128)) for m in range(8)]
        a = [[jnp.broadcast_to(c[j][i : i + 1, :], (8, 128)) if i >= j else None for j in range(8)] for i in range(8)]
        if not last:
            below = s_ref[lo + 8 : lo + 16, :]
            n = [jnp.broadcast_to(below[:, lo + m : lo + m + 1], (8, 128)) for m in range(8)]
        scale = jnp.zeros((8, 128), F32)
        for j in range(8):
            q = lax.rsqrt(a[j][j])
            r = q * q
            scale = jnp.where(sub == j, q, scale)
            w = [None] * 8
            for i in range(j + 1, 8):
                w[i] = a[i][j] * r
            for i in range(j + 1, 8):
                for m in range(j + 1, i + 1):
                    a[i][m] = a[i][m] - w[i] * a[m][j]
            unit = jnp.where(sub > j, c[j] * r, 0.0)
            for m in range(j + 1, 8):
                c[m] = c[m] - c[j] * w[m]
            pivot = jnp.broadcast_to(row[j : j + 1, :], (8, 256))
            row = row - jnp.concatenate([unit, unit], axis=1) * pivot
            if not last:
                lead = n[j] * r
                for m in range(j + 1, 8):
                    n[m] = n[m] - n[j] * w[m]
                below = below - jnp.concatenate([lead, lead], axis=1) * pivot
        done = row * jnp.concatenate([scale, scale], axis=1)
        u_ref[lo : lo + 8, :] = done
        before = done
        if not last:
            row = below


def factor_step(k, t_ref, s_ref, u_ref):
    rows = lax.broadcasted_iota(jnp.int32, (128, 128), 0)
    cols = lax.broadcasted_iota(jnp.int32, (128, 128), 1)
    base = pl.multiple_of(k * 128, 128)
    mine = pl.ds(base, 128)
    window = pl.ds(base, 640)

    def take(m, carry):
        above = pl.ds(pl.multiple_of(m * 128, 128), 128)
        t_ref[mine, window] = t_ref[mine, window] - tdot(t_ref[above, mine], t_ref[above, window])
        return carry

    lax.fori_loop(0, k, take, 0)
    s_ref[:, 0:128] = t_ref[mine, mine]
    s_ref[:, 128:256] = (rows == cols).astype(F32)
    factor_block(s_ref, u_ref)
    inverse = u_ref[:, 128:256]
    t_ref[mine, mine] = jnp.where(rows <= cols, u_ref[:, 0:128], 0.0)
    t_ref[mine, pl.ds(pl.multiple_of(base + 512, 128), 128)] = inverse
    middle = pl.ds(pl.multiple_of(base + 128, 128), 384)
    t_ref[mine, middle] = jnp.dot(inverse, t_ref[mine, middle], precision=HIGHEST, preferred_element_type=F32)


def gather_kernel(x_hbm, y_hbm, t_out, f_out, y_out, a_out, head, tile, other, hold, t_ref, s_ref, u_ref, sems, tree_recv, z_recv, d_recv, h_recv, t_recv, t_send, tree_send, z_send, d_send, pair_send, pair_recv):
    s = lax.axis_index("srow")
    z = lax.axis_index("scol")
    core = s % 2
    node = s // 2
    x = node % 4
    y = node // 4

    def at(px, py, pcore, pz):
        return (((py % 4) * 4 + px % 4) * 2 + pcore, pz)

    def remote(src, dst, send, recv, device):
        return pltpu.make_async_remote_copy(src_ref=src, dst_ref=dst, send_sem=send, recv_sem=recv, device_id=device, device_id_type=MESH)

    is_root = node == 0
    barrier = pltpu.get_barrier_semaphore()

    @pl.when(core == 1)
    def _():
        t_ref[...] = jnp.zeros_like(t_ref)

    def greet_plane(j, carry):
        pl.semaphore_signal(barrier, inc=1, device_id=((s + j) % 32, z), device_id_type=MESH)
        return carry

    def greet_line(j, carry):
        pl.semaphore_signal(barrier, inc=1, device_id=(s, (z + j) % 8), device_id_type=MESH)
        return carry

    lax.fori_loop(1, 32, greet_plane, 0)
    lax.fori_loop(1, 8, greet_line, 0)

    @pl.when(z == 0)
    def _():
        fetch = pltpu.make_async_copy(x_hbm.at[:, 0:8, :], head, sems.at[0])
        fetch.start()
        fetch.wait()
        for q in range(4):
            tile[:, 128 * q : 128 * q + 128] = head[:, q, :]

    pl.semaphore_wait(barrier, 38)

    def wide(k):
        return slice(128 * k, 512)

    mate = at(x, y, 1 - core, z)

    def flat(ref, n):
        return ref.at[pl.ds(n * 8, 8)]

    @pl.when(core == 1)
    def _():
        @pl.when(z == 0)
        def _():
            remote(tile, other, sems.at[1], sems.at[2], mate).start()
            pltpu.make_async_copy(tile, a_out, sems.at[3]).start()

        def step(k, carry):
            for j in range(4):

                @pl.when(k == j)
                def _():
                    rows = t_ref.at[128 * j : 128 * j + 128, wide(j)]
                    remote(rows, rows, d_send.at[j], d_recv.at[j], mate).wait_recv()

            factor_step(k, t_ref, s_ref, u_ref)
            block = pl.ds(pl.multiple_of(k * 128, 128), 128)
            remote(t_ref.at[block], t_out.at[block], t_send.at[k], t_recv.at[k], mate).start()
            pltpu.make_async_copy(t_ref.at[block], t_out.at[block], t_send.at[k + 4]).start()
            return carry

        lax.fori_loop(0, 4, step, 0)

        def drain(k, carry):
            block = pl.ds(pl.multiple_of(k * 128, 128), 128)
            remote(t_ref.at[block], t_out.at[block], t_send.at[k], t_recv.at[k], mate).wait_send()
            pltpu.make_async_copy(t_ref.at[block], t_out.at[block], t_send.at[k + 4]).wait()
            return carry

        lax.fori_loop(0, 4, drain, 0)
        remote(f_out, f_out, pair_send.at[0], pair_recv.at[0], mate).wait_recv()
        remote(y_out, y_out, pair_send.at[1], pair_recv.at[1], mate).wait_recv()

        @pl.when(z == 0)
        def _():
            remote(tile, other, sems.at[1], sems.at[2], mate).wait_send()
            pltpu.make_async_copy(tile, a_out, sems.at[3]).wait()

        @pl.when(z != 0)
        def _():
            remote(a_out, a_out, pair_send.at[2], pair_recv.at[2], mate).wait_recv()

    @pl.when(core == 0)
    def _():
        @pl.when(jnp.logical_and(is_root, z == 0))
        def _():
            for k in range(4):
                for q, (dx, dy) in enumerate(STEPS):
                    remote(tile.at[pl.ds(128 * k + 32 * q, 32), wide(k)], hold.at[k, :, wide(k)], d_send.at[k], h_recv.at[k], at(dx + 4, dy + 4, 0, 0)).start()

        for q, (dx, dy) in enumerate(STEPS):

            @pl.when(jnp.logical_and(x == dx % 4, y == dy % 4))
            def _():
                for k in range(4):
                    part = hold.at[k, :, wide(k)]
                    rows = pl.ds(128 * k + 32 * q, 32)
                    remote(part, part, d_send.at[k], h_recv.at[k], mate).wait_recv()

                    @pl.when(z == 0)
                    def _():
                        for far in (4, 3, 5, 2, 6, 1, 7):
                            remote(part, part, z_send.at[k + 4], h_recv.at[k], at(x, y, 0, far)).start()

                    def spread(j, carry):
                        remote(part, t_ref.at[rows, wide(k)], d_send.at[k], d_recv.at[k], at(x + (j + 2) % 4, y + (j // 4 + 2) % 4, 1, z)).start()
                        return carry

                    lax.fori_loop(0, 16, spread, 0)

        places = ((x, y), (y, 4 - x), (4 - x, 4 - y), (4 - y, x))
        starts = []
        gives = []
        for t in range(4):
            u = (places[t][1] % 4) * 4 + places[t][0] % 4
            depth = 0
            for n, d in enumerate(DEPTH):
                depth = depth + d * (u == n).astype(jnp.int32)
            starts.append(depth * HOP)
            mine = [None] * 4
            for d in range(4):
                hit = u == KIDS[d][0]
                for n in KIDS[d][1:]:
                    hit = jnp.logical_or(hit, u == n)
                mine[(d + t) % 4] = hit
            gives.append(mine)

        def pieces(t, n):
            return 256 * t + 16 * n, pl.multiple_of(128 * t + 16 * (n - 16), 16)

        def f_copy(src, t, n, send, recv, device):
            block = pl.ds(128 * t + 8 * n, 8)
            return remote(src.at[block], f_out.at[block], send, recv, device)

        def y_copy(src, t, n, send, recv, device):
            block = pl.ds(pl.multiple_of(128 * t + 16 * (n - 16), 16), 16)
            return remote(src.at[block], y_out.at[block], send, recv, device)

        def neighbour(d):
            return at(x + STEPS[d][0] + 4, y + STEPS[d][1] + 4, 0, z)

        def z_rows(i):
            return pl.ds(pl.multiple_of(32 * (i // 2), 32), 32)

        z_depth = jnp.minimum(z, 8 - z)
        z_up = z < 4
        z_down = jnp.logical_or(z == 0, z > 5)

        def z_step(i):
            for k in range(2):

                @pl.when(i % 2 == k)
                def _():
                    rows = z_rows(i)
                    dst = a_out if k == 0 else other

                    def send(src):
                        @pl.when(z_up)
                        def _():
                            remote(src.at[rows], dst.at[rows], z_send.at[k], z_recv.at[i], (s, (z + 1) % 8)).start()

                        @pl.when(z_down)
                        def _():
                            remote(src.at[rows], dst.at[rows], z_send.at[k + 2], z_recv.at[i], (s, (z + 7) % 8)).start()

                    @pl.when(z == 0)
                    def _():
                        send(tile if k == 0 else other)

                    @pl.when(z != 0)
                    def _():
                        remote(dst.at[rows], dst.at[rows], z_send.at[k], z_recv.at[i], mate).wait_recv()
                        send(dst)
                        if k == 1:
                            remote(other.at[rows], a_out.at[rows], pair_send.at[2], pair_recv.at[2], mate).start()

        @pl.when(z == 0)
        def _():
            remote(tile, other, sems.at[1], sems.at[2], mate).wait_recv()
            pltpu.make_async_copy(tile, a_out, sems.at[3]).start()

        def slot(i, carry):
            zi = i - HOP * z_depth

            @pl.when(jnp.logical_and(zi >= 0, zi < 32))
            def _():
                z_step(zi)

            @pl.when(is_root)
            def _():
                for t in range(4):

                    @pl.when(i < 16)
                    def _():
                        f_copy(x_hbm, t, i, tree_send.at[0, t], tree_recv.at[t, i], neighbour(t)).start()
                        f_copy(x_hbm, t, i, pair_send.at[0], pair_recv.at[0], mate).start()

                    @pl.when(jnp.logical_and(i >= 16, i < CHUNKS))
                    def _():
                        y_copy(y_hbm, t, i, tree_send.at[1, t], tree_recv.at[t, i], neighbour(t)).start()
                        y_copy(y_hbm, t, i, pair_send.at[1], pair_recv.at[1], mate).start()

            @pl.when(jnp.logical_not(is_root))
            def _():
                for t in range(4):
                    n = i - starts[t]

                    @pl.when(jnp.logical_and(n >= 0, n < 16))
                    def _():
                        f_copy(f_out, t, n, tree_send.at[0, 0], tree_recv.at[t, n], mate).wait_recv()
                        for d in range(4):

                            @pl.when(gives[t][d])
                            def _():
                                f_copy(f_out, t, n, tree_send.at[0, 4 * t + d], tree_recv.at[t, n], neighbour(d)).start()

                        f_copy(f_out, t, n, pair_send.at[0], pair_recv.at[0], mate).start()

                    @pl.when(jnp.logical_and(n >= 16, n < CHUNKS))
                    def _():
                        y_copy(y_out, t, n, tree_send.at[1, 0], tree_recv.at[t, n], mate).wait_recv()
                        for d in range(4):

                            @pl.when(gives[t][d])
                            def _():
                                y_copy(y_out, t, n, tree_send.at[1, 4 * t + d], tree_recv.at[t, n], neighbour(d)).start()

                        y_copy(y_out, t, n, pair_send.at[1], pair_recv.at[1], mate).start()

            return carry

        lax.fori_loop(0, CHUNKS + 6 * HOP, slot, 0)

        def f_sent(send):
            part = f_out.at[pl.ds(0, 128)]
            remote(part, part, send, pair_recv.at[0], mate).wait_send()

        def y_sent(send):
            part = y_out.at[pl.ds(0, 128)]
            remote(part, part, send, pair_recv.at[1], mate).wait_send()

        @pl.when(is_root)
        def _():
            for t in range(4):
                f_sent(tree_send.at[0, t])
                y_sent(tree_send.at[1, t])

        @pl.when(jnp.logical_not(is_root))
        def _():
            for t in range(4):
                for d in range(4):

                    @pl.when(gives[t][d])
                    def _():
                        f_sent(tree_send.at[0, 4 * t + d])
                        y_sent(tree_send.at[1, 4 * t + d])

        remote(f_out, f_out, pair_send.at[0], pair_recv.at[0], mate).wait_send()
        remote(y_out, y_out, pair_send.at[1], pair_recv.at[1], mate).wait_send()
        for k in range(2):

            @pl.when(z_up)
            def _():
                remote(a_out, a_out, z_send.at[k], pair_recv.at[2], mate).wait_send()

            @pl.when(z_down)
            def _():
                remote(a_out, a_out, z_send.at[k + 2], pair_recv.at[2], mate).wait_send()

        @pl.when(z == 0)
        def _():
            pltpu.make_async_copy(tile, a_out, sems.at[3]).wait()

        @pl.when(z != 0)
        def _():
            remote(a_out, a_out, pair_send.at[2], pair_recv.at[2], mate).wait_send()

        @pl.when(jnp.logical_and(is_root, z == 0))
        def _():
            for k in range(4):
                part = tile.at[0:128, wide(k)]
                remote(part, part, d_send.at[k], h_recv.at[k], mate).wait_send()

        for q, (dx, dy) in enumerate(STEPS):

            @pl.when(jnp.logical_and(x == dx % 4, y == dy % 4))
            def _():
                for k in range(4):
                    part = tile.at[:, wide(k)]
                    remote(part, part, d_send.at[k], h_recv.at[k], mate).wait_send()

                    @pl.when(z == 0)
                    def _():
                        part = tile.at[0:224, wide(k)]
                        remote(part, part, z_send.at[k + 4], h_recv.at[k], mate).wait_send()

        def due(k, carry):
            block = pl.ds(pl.multiple_of(k * 128, 128), 128)
            remote(t_out.at[block], t_out.at[block], t_send.at[k], t_recv.at[k], mate).wait_recv()
            return carry

        lax.fori_loop(0, 4, due, 0)


def gather(x, y):
    dma = pltpu.SemaphoreType.DMA
    anyspace = pl.BlockSpec(memory_space=pl.ANY)
    return pl.pallas_call(
        gather_kernel,
        out_shape=(
            jax.ShapeDtypeStruct((512, 1024), F32),
            jax.ShapeDtypeStruct((512, 16, 128), F32),
            jax.ShapeDtypeStruct((512, 1024), F32),
            jax.ShapeDtypeStruct((512, 512), F32),
        ),
        in_specs=[anyspace] * 2,
        out_specs=[anyspace] * 4,
        scratch_shapes=[
            pltpu.VMEM((512, 8, 128), F32),
            pltpu.VMEM((512, 512), F32),
            pltpu.VMEM((512, 512), F32),
            pltpu.VMEM((4, 32, 512), F32),
            pltpu.VMEM((512, 1024), F32),
            pltpu.VMEM((128, 256), F32),
            pltpu.VMEM((128, 256), F32),
            dma((4,)),
            dma((4, CHUNKS)),
            dma((32,)),
            dma((4,)),
            dma((4,)),
            dma((4,)),
            dma((8,)),
            dma((2, 16)),
            dma((8,)),
            dma((4,)),
            dma((3,)),
            dma((3,)),
        ],
        compiler_params=pltpu.CompilerParams(collective_id=0, has_side_effects=True, vmem_limit_bytes=32 << 20),
        name="gather",
    )(x, y)


def split(v):
    high = v.astype(BF16)
    return high, (v - high.astype(F32)).astype(BF16)


def dot3(a, b):
    ah, al = a
    bh, bl = b
    dot = functools.partial(jnp.dot, preferred_element_type=F32)
    return dot(ah, bh) + (dot(ah, bl) + dot(al, bh))


def update_kernel(t_hbm, f_hbm, r_hbm, a_hbm, x_hbm, y_hbm, fo_hbm, yo_hbm, t, a, f, r, x, y, fo, yo, sems):
    s = lax.axis_index("srow")
    z = lax.axis_index("scol")
    loads = [
        pltpu.make_async_copy(src, dst, sems.at[i])
        for i, (src, dst) in enumerate(((t_hbm, t), (a_hbm, a), (f_hbm, f), (x_hbm, x), (r_hbm, r), (y_hbm, y)))
    ]
    stores = [pltpu.make_async_copy(src, dst, sems.at[6 + i]) for i, (src, dst) in enumerate(((fo, fo_hbm), (yo, yo_hbm)))]
    for load in loads:
        load.start()
    loads[0].wait()
    loads[1].wait()

    def lane(ref, i):
        return ref.at[pl.ds(i, 512, stride=16), :]

    @pl.when(s != 0)
    def _():
        inverse = t[:, 512:1024]
        panel = lax.dot_general(a[...], inverse, (((1,), (1,)), ((), ())), precision=HIGHEST, preferred_element_type=F32)
        q = split(jnp.dot(panel, inverse, precision=HIGHEST, preferred_element_type=F32))
        loads[2].wait()
        loads[3].wait()
        for c in range(4):
            right = split(jnp.concatenate([lane(f, 4 * c + j)[...] for j in range(4)], axis=1))
            change = dot3(q, right)
            for j in range(4):
                lane(fo, 4 * c + j)[...] = lane(x, 4 * c + j)[...] - change[:, 128 * j : 128 * j + 128]

        @pl.when(z == 0)
        def _():
            for j in range(4):
                lane(fo, j)[...] = panel[:, 128 * j : 128 * j + 128]

        stores[0].start()
        loads[4].wait()
        loads[5].wait()
        for c in range(2):
            part = slice(512 * c, 512 * c + 512)
            yo[:, part] = y[:, part] - dot3(q, split(r[:, part]))
        stores[1].start()

    @pl.when(s == 0)
    def _():
        fo[...] = jnp.zeros_like(fo)

        @pl.when(z == 0)
        def _():
            rows = lax.broadcasted_iota(jnp.int32, (512, 512), 0)
            cols = lax.broadcasted_iota(jnp.int32, (512, 512), 1)
            lower = jnp.where(rows >= cols, t[:, 0:512].T, 0.0)
            for j in range(4):
                lane(fo, j)[...] = lower[:, 128 * j : 128 * j + 128]

        stores[0].start()
        for load in loads[2:]:
            load.wait()
        yo[...] = jnp.dot(t[:, 512:1024], y[...], precision=HIGHEST, preferred_element_type=F32)
        stores[1].start()

    stores[0].wait()
    stores[1].wait()


def update(t, f, r, a, x, y):
    anyspace = pl.BlockSpec(memory_space=pl.ANY)
    return pl.pallas_call(
        update_kernel,
        out_shape=(jax.ShapeDtypeStruct((8192, 128), F32), jax.ShapeDtypeStruct((512, 1024), F32)),
        in_specs=[anyspace] * 6,
        out_specs=[anyspace] * 2,
        scratch_shapes=[
            pltpu.VMEM((512, 1024), F32),
            pltpu.VMEM((512, 512), F32),
            pltpu.VMEM((8192, 128), F32),
            pltpu.VMEM((512, 1024), F32),
            pltpu.VMEM((8192, 128), F32),
            pltpu.VMEM((512, 1024), F32),
            pltpu.VMEM((8192, 128), F32),
            pltpu.VMEM((512, 1024), F32),
            pltpu.SemaphoreType.DMA((8,)),
        ],
        compiler_params=pltpu.CompilerParams(vmem_limit_bytes=48 << 20),
        name="update",
    )(t, f, r, a, x, y)


def per_device(factor_state, data):
    x = factor_state.reshape(512, 16, 128)
    y = data.reshape(512, 1024)
    t, f, r, a = gather(x, y)
    factor_out, data_out = update(t, f.reshape(8192, 128), r, a, x.reshape(8192, 128), y)
    return factor_out.reshape(factor_state.shape), data_out.reshape(data.shape)


def solution(mesh):
    specs = (P("srow", None, None, "scol", None), P("srow", None, "scol"))
    return jax.shard_map(per_device, mesh=mesh, in_specs=specs, out_specs=specs, check_vma=False)
```

```python
import functools

import jax
import jax.numpy as jnp
from jax import lax
from jax.experimental import pallas as pl
from jax.experimental.pallas import tpu as pltpu
from jax.sharding import PartitionSpec as P

F32 = jnp.float32
BF16 = jnp.bfloat16
HIGHEST = lax.Precision.HIGHEST
MESH = pl.DeviceIdType.MESH
STEPS = ((1, 0), (0, 1), (-1, 0), (0, -1))
DEPTH = (0, 1, 2, 3, 3, 2, 3, 4, 4, 3, 4, 5, 3, 2, 3, 4)
KIDS = ((0, 1, 2, 5, 6, 10, 14), (1, 5), (5, 9, 13), (1, 2, 14))
HOP = 4
CHUNKS = 24


def tdot(a, b):
    return lax.dot_general(a, b, (((0,), (0,)), ((), ())), precision=HIGHEST, preferred_element_type=F32)


def factor_block(s_ref, u_ref):
    sub = lax.broadcasted_iota(jnp.int32, (8, 128), 0)
    row = s_ref[0:8, :]
    before = None
    for k in range(16):
        lo = 8 * k
        last = k == 15
        if before is not None and not last:
            s_ref[lo + 8 : 128, :] = s_ref[lo + 8 : 128, :] - tdot(before[:, lo + 8 : 128], before)
        c = [jnp.broadcast_to(row[:, lo + m : lo + m + 1], (8, 128)) for m in range(8)]
        a = [[jnp.broadcast_to(c[j][i : i + 1, :], (8, 128)) if i >= j else None for j in range(8)] for i in range(8)]
        if not last:
            below = s_ref[lo + 8 : lo + 16, :]
            n = [jnp.broadcast_to(below[:, lo + m : lo + m + 1], (8, 128)) for m in range(8)]
        scale = jnp.zeros((8, 128), F32)
        for j in range(8):
            q = lax.rsqrt(a[j][j])
            r = q * q
            scale = jnp.where(sub == j, q, scale)
            w = [None] * 8
            for i in range(j + 1, 8):
                w[i] = a[i][j] * r
            for i in range(j + 1, 8):
                for m in range(j + 1, i + 1):
                    a[i][m] = a[i][m] - w[i] * a[m][j]
            unit = jnp.where(sub > j, c[j] * r, 0.0)
            for m in range(j + 1, 8):
                c[m] = c[m] - c[j] * w[m]
            pivot = jnp.broadcast_to(row[j : j + 1, :], (8, 256))
            row = row - jnp.concatenate([unit, unit], axis=1) * pivot
            if not last:
                lead = n[j] * r
                for m in range(j + 1, 8):
                    n[m] = n[m] - n[j] * w[m]
                below = below - jnp.concatenate([lead, lead], axis=1) * pivot
        done = row * jnp.concatenate([scale, scale], axis=1)
        u_ref[lo : lo + 8, :] = done
        before = done
        if not last:
            row = below


def gather_kernel(x_hbm, y_hbm, t_out, f_out, y_out, a_out, head, tile, other, hold, t_ref, s_ref, u_ref, sems, tree_recv, root_recv, z_recv, h_recv, d_recv, t_recv, t_send, r_send, l_send, d_send, c_send, tree_send, root_send, z_send, pair_send, pair_recv):
    s = lax.axis_index("srow")
    z = lax.axis_index("scol")
    core = s % 2
    node = s // 2
    x = node % 4
    y = node // 4
    is_root = node == 0
    is_first = jnp.logical_and(s == 0, z == 0)

    def at(px, py, pcore, pz):
        return (((py % 4) * 4 + px % 4) * 2 + pcore, pz)

    def remote(src, dst, send, recv, device):
        return pltpu.make_async_remote_copy(src_ref=src, dst_ref=dst, send_sem=send, recv_sem=recv, device_id=device, device_id_type=MESH)

    mate = at(x, y, 1 - core, z)
    barrier = pltpu.get_barrier_semaphore()

    def greet_plane(j, carry):
        pl.semaphore_signal(barrier, inc=1, device_id=((s + j) % 32, z), device_id_type=MESH)
        return carry

    def greet_line(j, carry):
        pl.semaphore_signal(barrier, inc=1, device_id=(s, (z + j) % 8), device_id_type=MESH)
        return carry

    lax.fori_loop(1, 32, greet_plane, 0)
    lax.fori_loop(1, 8, greet_line, 0)

    @pl.when(z == 0)
    def _():
        fetch = pltpu.make_async_copy(x_hbm.at[:, 0:8, :], head, sems.at[0])
        fetch.start()
        fetch.wait()
        for q in range(4):
            tile[:, 128 * q : 128 * q + 128] = head[:, q, :]

    pieces = []
    for k in range(4):
        if k:
            pieces.append((k, 0, 128 * k))
        pieces.append((k, 128 * k, 128))

    def piece_rows(k, q):
        return pl.ds(pl.multiple_of(128 * k + 32 * q, 32), 32)

    def lanes(p, shift=0):
        return slice(pieces[p][1] + shift, pieces[p][1] + pieces[p][2] + shift)

    def hand_over():
        for g in range(4):
            for t in range(4):
                block = slice(128 * t + 32 * g, 128 * t + 32 * g + 32)
                copy = remote(x_hbm.at[block], f_out.at[block], pair_send.at[0], root_recv.at[t, g], mate)
                copy.start()
        for g in range(2):
            for t in range(4):
                block = slice(128 * t + 64 * g, 128 * t + 64 * g + 64)
                copy = remote(y_hbm.at[block], y_out.at[block], pair_send.at[1], root_recv.at[t, g + 4], mate)
                copy.start()

    def give_tile():
        remote(tile, other, sems.at[1], sems.at[2], mate).start()
        pltpu.make_async_copy(tile, a_out, sems.at[3]).start()

    @pl.when(is_first)
    def _():
        t_ref[:, 0:512] = tile[...]
        t_ref[:, 512:1024] = jnp.zeros((512, 512), F32)
        rows = lax.broadcasted_iota(jnp.int32, (128, 128), 0)
        cols = lax.broadcasted_iota(jnp.int32, (128, 128), 1)

        def give(p):
            k = pieces[p][0]
            for q, (dx, dy) in enumerate(STEPS):
                remote(t_ref.at[128 * k + 32 * q : 128 * k + 32 * q + 32, lanes(p, 512)], hold.at[k, :, lanes(p)], r_send.at[p], h_recv.at[p], at(dx + 4, dy + 4, 0, 0)).start()

        def given(p):
            part = t_ref.at[0:128, lanes(p, 512)]
            remote(part, part, r_send.at[p], h_recv.at[p], mate).wait_send()

        def step(k, carry):
            base = pl.multiple_of(k * 128, 128)
            mine = pl.ds(base, 128)
            s_ref[:, 0:128] = t_ref[mine, mine]
            s_ref[:, 128:256] = (rows == cols).astype(F32)
            factor_block(s_ref, u_ref)
            inverse = u_ref[:, 128:256]
            t_ref[mine, mine] = jnp.where(rows <= cols, u_ref[:, 0:128], 0.0)
            t_ref[mine, pl.ds(pl.multiple_of(base + 512, 128), 128)] = inverse

            @pl.when(k == 0)
            def _():
                pl.semaphore_wait(barrier, 38)

            for j in range(4):

                @pl.when(k == j)
                def _():
                    give(2 * j)
                    if j:
                        given(2 * j - 1)

            @pl.when(k == 0)
            def _():
                give_tile()
                hand_over()

            middle = pl.ds(pl.multiple_of(base + 128, 128), 384)
            t_ref[mine, middle] = jnp.dot(inverse, t_ref[mine, middle], precision=HIGHEST, preferred_element_type=F32)

            @pl.when(k < 3)
            def _():
                later = pl.multiple_of(base + 128, 128)
                coming = pl.ds(later, 128)
                window = pl.ds(later, 640)

                def take(m, inner):
                    above = pl.ds(pl.multiple_of(m * 128, 128), 128)
                    t_ref[coming, window] = t_ref[coming, window] - tdot(t_ref[above, coming], t_ref[above, window])
                    return inner

                lax.fori_loop(0, k + 1, take, 0)

            for j in range(3):

                @pl.when(k == j)
                def _():
                    give(2 * j + 1)

            return carry

        lax.fori_loop(0, 4, step, 0)
        keep = pltpu.make_async_copy(t_ref.at[:, 0:512], t_out.at[:, 0:512], sems.at[0])
        keep.start()
        for j in range(4):
            given(2 * j)
        keep.wait()

    @pl.when(jnp.logical_not(is_first))
    def _():
        pl.semaphore_wait(barrier, 38)

        @pl.when(z == 0)
        def _():
            give_tile()

        @pl.when(s == 0)
        def _():
            hand_over()

    @pl.when(core == 0)
    def _():
        quarter = jnp.where(x == 1, 0, jnp.where(y == 1, 1, jnp.where(x == 3, 2, 3)))
        holder = jnp.logical_or(jnp.logical_and(y == 0, x % 2 == 1), jnp.logical_and(x == 0, y % 2 == 1))

        @pl.when(holder)
        def _():
            for p, (k, _, _) in enumerate(pieces):
                part = hold.at[k, :, lanes(p)]
                mine = t_out.at[piece_rows(k, quarter), lanes(p, 512)]
                remote(part, part, r_send.at[p], h_recv.at[p], mate).wait_recv()

                @pl.when(z == 0)
                def _():
                    for far in (4, 3, 5, 2, 6, 1, 7):
                        remote(part, part, l_send.at[p], h_recv.at[p], (s, far)).start()

                def around(j, carry):
                    remote(part, mine, d_send.at[p], d_recv.at[p], ((s + 2 * j) % 32, z)).start()
                    return carry

                lax.fori_loop(1, 16, around, 0)
                pltpu.make_async_copy(part, mine, c_send.at[p]).start()

        for p, (k, _, _) in enumerate(pieces):

            @pl.when(holder)
            def _():
                part = t_out.at[0:96, lanes(p, 512)]
                remote(part, part, d_send.at[p], d_recv.at[p], mate).wait_recv()
                pltpu.make_async_copy(hold.at[k, :, lanes(p)], t_out.at[piece_rows(k, quarter), lanes(p, 512)], c_send.at[p]).wait()

            whole = t_out.at[128 * k : 128 * k + 128, lanes(p, 512)]

            @pl.when(jnp.logical_not(holder))
            def _():
                remote(whole, whole, d_send.at[p], d_recv.at[p], mate).wait_recv()

            remote(whole, whole, t_send.at[p], t_recv.at[p], mate).start()

        for p, (k, _, _) in enumerate(pieces):
            whole = t_out.at[128 * k : 128 * k + 128, lanes(p, 512)]
            remote(whole, whole, t_send.at[p], t_recv.at[p], mate).wait_send()

            @pl.when(holder)
            def _():
                part = t_ref.at[0:480, lanes(p)]
                remote(part, part, d_send.at[p], d_recv.at[p], mate).wait_send()

                @pl.when(z == 0)
                def _():
                    part = t_ref.at[0:224, lanes(p)]
                    remote(part, part, l_send.at[p], h_recv.at[p], mate).wait_send()

        @pl.when(z == 0)
        def _():
            remote(tile, other, sems.at[1], sems.at[2], mate).wait_recv()
            remote(tile, other, sems.at[1], sems.at[2], mate).wait_send()
            pltpu.make_async_copy(tile, a_out, sems.at[3]).wait()

        @pl.when(z != 0)
        def _():
            remote(a_out, a_out, pair_send.at[2], pair_recv.at[2], mate).wait_recv()

        @pl.when(is_root)
        def _():
            remote(f_out, f_out, pair_send.at[0], pair_recv.at[0], mate).wait_send()
            remote(y_out, y_out, pair_send.at[1], pair_recv.at[1], mate).wait_send()

        @pl.when(jnp.logical_not(is_root))
        def _():
            remote(f_out, f_out, pair_send.at[0], pair_recv.at[0], mate).wait_recv()
            remote(y_out, y_out, pair_send.at[1], pair_recv.at[1], mate).wait_recv()

    @pl.when(core == 1)
    def _():
        places = ((x, y), (y, 4 - x), (4 - x, 4 - y), (4 - y, x))
        starts = []
        gives = []
        for t in range(4):
            u = (places[t][1] % 4) * 4 + places[t][0] % 4
            depth = 0
            for n, d in enumerate(DEPTH):
                depth = depth + d * (u == n).astype(jnp.int32)
            starts.append(depth * HOP)
            mine = [None] * 4
            for d in range(4):
                hit = u == KIDS[d][0]
                for n in KIDS[d][1:]:
                    hit = jnp.logical_or(hit, u == n)
                mine[(d + t) % 4] = hit
            gives.append(mine)

        def f_copy(t, n, send, recv, device):
            block = f_out.at[pl.ds(128 * t + 8 * n, 8)]
            return remote(block, block, send, recv, device)

        def y_copy(t, n, send, recv, device):
            block = y_out.at[pl.ds(pl.multiple_of(128 * t + 16 * n, 16), 16)]
            return remote(block, block, send, recv, device)

        def neighbour(d):
            return at(x + STEPS[d][0] + 4, y + STEPS[d][1] + 4, 1, z)

        z_depth = jnp.minimum(z, 8 - z)
        z_up = z < 4
        z_down = jnp.logical_or(z == 0, z > 5)

        def z_step(i):
            for k in range(2):

                @pl.when(i % 2 == k)
                def _():
                    rows = pl.ds(pl.multiple_of(32 * (i // 2), 32), 32)
                    dst = a_out if k == 0 else other

                    def send(src):
                        @pl.when(z_up)
                        def _():
                            remote(src.at[rows], dst.at[rows], z_send.at[k], z_recv.at[i], (s, (z + 1) % 8)).start()

                        @pl.when(z_down)
                        def _():
                            remote(src.at[rows], dst.at[rows], z_send.at[k + 2], z_recv.at[i], (s, (z + 7) % 8)).start()

                    @pl.when(z == 0)
                    def _():
                        send(tile if k == 0 else other)

                    @pl.when(z != 0)
                    def _():
                        remote(dst.at[rows], dst.at[rows], z_send.at[k], z_recv.at[i], mate).wait_recv()
                        send(dst)
                        if k == 1:
                            remote(other.at[rows], a_out.at[rows], pair_send.at[2], pair_recv.at[2], mate).start()

        def flow(kind, t, n, copy, total, part):
            @pl.when(is_root)
            def _():
                @pl.when(n % (total // part) == 0)
                def _():
                    if kind == 0:
                        block = f_out.at[0:32]
                    else:
                        block = y_out.at[0:64]
                    remote(block, block, pair_send.at[kind], root_recv.at[t, 4 * kind + n // (total // part)], mate).wait_recv()

                @pl.when(n >= 2)
                def _():
                    copy(t, n, root_send.at[kind, t, n % 2], tree_recv.at[t, n + 16 * kind], neighbour(t)).wait_send()

                copy(t, n, root_send.at[kind, t, n % 2], tree_recv.at[t, n + 16 * kind], neighbour(t)).start()

            @pl.when(jnp.logical_not(is_root))
            def _():
                copy(t, n, tree_send.at[kind, 0], tree_recv.at[t, n + 16 * kind], mate).wait_recv()
                for d in range(4):

                    @pl.when(gives[t][d])
                    def _():
                        copy(t, n, tree_send.at[kind, 4 * t + d], tree_recv.at[t, n + 16 * kind], neighbour(d)).start()

                copy(t, n, pair_send.at[kind], pair_recv.at[kind], mate).start()

        def slot(i, carry):
            for t in range(4):
                n = i - starts[t]

                @pl.when(jnp.logical_and(n >= 0, n < 16))
                def _():
                    flow(0, t, n, f_copy, 16, 4)

                @pl.when(jnp.logical_and(n >= 16, n < CHUNKS))
                def _():
                    flow(1, t, n - 16, y_copy, 8, 2)

            zi = i - HOP * z_depth - 4

            @pl.when(jnp.logical_and(z == 0, zi == 0))
            def _():
                remote(tile, other, sems.at[1], sems.at[2], mate).wait_recv()

            @pl.when(jnp.logical_and(zi >= 0, zi < 32))
            def _():
                z_step(zi)

            return carry

        lax.fori_loop(0, 36 + 4 * HOP, slot, 0)

        f_part = f_out.at[0:128]
        y_part = y_out.at[0:128]

        @pl.when(is_root)
        def _():
            for t in range(4):
                for j in range(2):
                    f_copy(t, j, root_send.at[0, t, j], tree_recv.at[t, 0], mate).wait_send()
                    y_copy(t, j, root_send.at[1, t, j], tree_recv.at[t, 0], mate).wait_send()

        @pl.when(jnp.logical_not(is_root))
        def _():
            for t in range(4):
                for d in range(4):

                    @pl.when(gives[t][d])
                    def _():
                        remote(f_part, f_part, tree_send.at[0, 4 * t + d], pair_recv.at[0], mate).wait_send()
                        remote(y_part, y_part, tree_send.at[1, 4 * t + d], pair_recv.at[1], mate).wait_send()

            remote(f_out, f_out, pair_send.at[0], pair_recv.at[0], mate).wait_send()
            remote(y_out, y_out, pair_send.at[1], pair_recv.at[1], mate).wait_send()

        for k in range(2):

            @pl.when(z_up)
            def _():
                remote(a_out, a_out, z_send.at[k], pair_recv.at[2], mate).wait_send()

            @pl.when(z_down)
            def _():
                remote(a_out, a_out, z_send.at[k + 2], pair_recv.at[2], mate).wait_send()

        @pl.when(z == 0)
        def _():
            remote(tile, other, sems.at[1], sems.at[2], mate).wait_send()
            pltpu.make_async_copy(tile, a_out, sems.at[3]).wait()

        @pl.when(z != 0)
        def _():
            remote(a_out, a_out, pair_send.at[2], pair_recv.at[2], mate).wait_send()

        for p, (k, _, _) in enumerate(pieces):
            whole = t_out.at[128 * k : 128 * k + 128, lanes(p, 512)]
            remote(whole, whole, t_send.at[p], t_recv.at[p], mate).wait_recv()


def gather(x, y):
    dma = pltpu.SemaphoreType.DMA
    anyspace = pl.BlockSpec(memory_space=pl.ANY)
    return pl.pallas_call(
        gather_kernel,
        out_shape=(
            jax.ShapeDtypeStruct((512, 1024), F32),
            jax.ShapeDtypeStruct((512, 16, 128), F32),
            jax.ShapeDtypeStruct((512, 1024), F32),
            jax.ShapeDtypeStruct((512, 512), F32),
        ),
        in_specs=[pl.BlockSpec(memory_space=pltpu.HBM)] * 2,
        out_specs=[anyspace] * 4,
        scratch_shapes=[
            pltpu.VMEM((512, 8, 128), F32),
            pltpu.VMEM((512, 512), F32),
            pltpu.VMEM((512, 512), F32),
            pltpu.VMEM((4, 32, 512), F32),
            pltpu.VMEM((512, 1024), F32),
            pltpu.VMEM((128, 256), F32),
            pltpu.VMEM((128, 256), F32),
            dma((4,)),
            dma((4, CHUNKS)),
            dma((4, 6)),
            dma((32,)),
            dma((7,)),
            dma((7,)),
            dma((7,)),
            dma((7,)),
            dma((7,)),
            dma((7,)),
            dma((7,)),
            dma((7,)),
            dma((2, 16)),
            dma((2, 4, 2)),
            dma((4,)),
            dma((3,)),
            dma((3,)),
        ],
        compiler_params=pltpu.CompilerParams(collective_id=0, has_side_effects=True, vmem_limit_bytes=60 << 20),
        name="gather",
    )(x, y)


def split(v):
    high = v.astype(BF16)
    return high, (v - high.astype(F32)).astype(BF16)


def dot3(a, b, dims=(((1,), (0,)), ((), ()))):
    ah, al = a
    bh, bl = b
    dot = functools.partial(lax.dot_general, dimension_numbers=dims, preferred_element_type=F32)
    return dot(ah, bh) + (dot(ah, bl) + dot(al, bh))


def update_kernel(t_hbm, f_hbm, r_hbm, a_hbm, x_hbm, y_hbm, fo_hbm, yo_hbm, t, a, f, r, x, y, fo, yo, p, q_ref, sems):
    s = lax.axis_index("srow")
    z = lax.axis_index("scol")
    loads = [
        pltpu.make_async_copy(src, dst, sems.at[i])
        for i, (src, dst) in enumerate(((t_hbm, t), (a_hbm, a), (f_hbm, f), (x_hbm, x), (r_hbm, r), (y_hbm, y)))
    ]
    stores = [pltpu.make_async_copy(src, dst, sems.at[6 + i]) for i, (src, dst) in enumerate(((fo, fo_hbm), (yo, yo_hbm)))]
    for load in loads:
        load.start()
    loads[0].wait()
    loads[1].wait()

    def lane(ref, i):
        return ref.at[pl.ds(i, 512, stride=16), :]

    def inverse_rows(k):
        rows = slice(128 * k, 128 * k + 128)
        own = t[rows, 512 + 128 * k : 640 + 128 * k]
        if k == 0:
            return own
        left = jnp.dot(own, t[rows, 512 : 512 + 128 * k], precision=HIGHEST, preferred_element_type=F32)
        return jnp.concatenate([left, own], axis=1)

    @pl.when(s != 0)
    def _():
        al = split(a[...])
        for k in range(4):
            width = 128 * k + 128
            xs = split(inverse_rows(k))
            panel = dot3((al[0][:, :width], al[1][:, :width]), xs, (((1,), (1,)), ((), ())))
            p[:, 128 * k : width] = panel
            add = dot3(split(panel), xs)
            if k:
                q_ref[:, : 128 * k] = q_ref[:, : 128 * k] + add[:, : 128 * k]
            q_ref[:, 128 * k : width] = add[:, 128 * k :]
        q = split(q_ref[...])
        loads[2].wait()
        loads[3].wait()
        for c in range(4):
            right = split(jnp.concatenate([lane(f, 4 * c + j)[...] for j in range(4)], axis=1))
            change = dot3(q, right)
            for j in range(4):
                lane(fo, 4 * c + j)[...] = lane(x, 4 * c + j)[...] - change[:, 128 * j : 128 * j + 128]

        @pl.when(z == 0)
        def _():
            for j in range(4):
                lane(fo, j)[...] = p[:, 128 * j : 128 * j + 128]

        stores[0].start()
        loads[4].wait()
        loads[5].wait()
        for c in range(2):
            part = slice(512 * c, 512 * c + 512)
            yo[:, part] = y[:, part] - dot3(q, split(r[:, part]))
        stores[1].start()

    @pl.when(s == 0)
    def _():
        fo[...] = jnp.zeros_like(fo)

        @pl.when(z == 0)
        def _():
            rows = lax.broadcasted_iota(jnp.int32, (512, 512), 0)
            cols = lax.broadcasted_iota(jnp.int32, (512, 512), 1)
            lower = jnp.where(rows >= cols, t[:, 0:512].T, 0.0)
            for j in range(4):
                lane(fo, j)[...] = lower[:, 128 * j : 128 * j + 128]

        stores[0].start()
        for load in loads[2:]:
            load.wait()
        ys = split(y[...])
        for k in range(4):
            width = 128 * k + 128
            yo[128 * k : width, :] = dot3(split(inverse_rows(k)), (ys[0][:width], ys[1][:width]))
        stores[1].start()

    stores[0].wait()
    stores[1].wait()


def update(t, f, r, a, x, y):
    anyspace = pl.BlockSpec(memory_space=pl.ANY)
    return pl.pallas_call(
        update_kernel,
        out_shape=(jax.ShapeDtypeStruct((8192, 128), F32), jax.ShapeDtypeStruct((512, 1024), F32)),
        in_specs=[anyspace] * 6,
        out_specs=[anyspace] * 2,
        scratch_shapes=[
            pltpu.VMEM((512, 1024), F32),
            pltpu.VMEM((512, 512), F32),
            pltpu.VMEM((8192, 128), F32),
            pltpu.VMEM((512, 1024), F32),
            pltpu.VMEM((8192, 128), F32),
            pltpu.VMEM((512, 1024), F32),
            pltpu.VMEM((8192, 128), F32),
            pltpu.VMEM((512, 1024), F32),
            pltpu.VMEM((512, 512), F32),
            pltpu.VMEM((512, 512), F32),
            pltpu.SemaphoreType.DMA((8,)),
        ],
        compiler_params=pltpu.CompilerParams(vmem_limit_bytes=60 << 20),
        name="update",
    )(t, f, r, a, x, y)


def per_device(factor_state, data):
    x = factor_state.reshape(512, 16, 128)
    y = data.reshape(512, 1024)
    t, f, r, a = gather(x, y)
    factor_out, data_out = update(t, f.reshape(8192, 128), r, a, x.reshape(8192, 128), y)
    return factor_out.reshape(factor_state.shape), data_out.reshape(data.shape)


def solution(mesh):
    specs = (P("srow", None, None, "scol", None), P("srow", None, "scol"))
    return jax.shard_map(per_device, mesh=mesh, in_specs=specs, out_specs=specs, check_vma=False)
```

```python
import functools

import jax
import jax.numpy as jnp
from jax import lax
from jax.experimental import pallas as pl
from jax.experimental.pallas import tpu as pltpu
from jax.sharding import PartitionSpec as P

F32 = jnp.float32
BF16 = jnp.bfloat16
HIGHEST = lax.Precision.HIGHEST
MESH = pl.DeviceIdType.MESH
STEPS = ((1, 0), (0, 1), (-1, 0), (0, -1))
DEPTH = (0, 1, 2, 3, 3, 2, 3, 4, 4, 3, 4, 5, 3, 2, 3, 4)
KIDS = ((0, 1, 2, 5, 6, 10, 14), (1, 5), (5, 9, 13), (1, 2, 14))
HOP = 4
CHUNKS = 24


def tdot(a, b):
    return lax.dot_general(a, b, (((0,), (0,)), ((), ())), precision=HIGHEST, preferred_element_type=F32)


def factor_block(s_ref, u_ref):
    sub = lax.broadcasted_iota(jnp.int32, (8, 128), 0)
    row = s_ref[0:8, :]
    before = None
    for k in range(16):
        lo = 8 * k
        last = k == 15
        if before is not None and not last:
            s_ref[lo + 8 : 128, :] = s_ref[lo + 8 : 128, :] - tdot(before[:, lo + 8 : 128], before)
        c = [jnp.broadcast_to(row[:, lo + m : lo + m + 1], (8, 128)) for m in range(8)]
        a = [[jnp.broadcast_to(c[j][i : i + 1, :], (8, 128)) if i >= j else None for j in range(8)] for i in range(8)]
        if not last:
            below = s_ref[lo + 8 : lo + 16, :]
            n = [jnp.broadcast_to(below[:, lo + m : lo + m + 1], (8, 128)) for m in range(8)]
        scale = jnp.zeros((8, 128), F32)
        for j in range(8):
            q = lax.rsqrt(a[j][j])
            r = q * q
            scale = jnp.where(sub == j, q, scale)
            w = [None] * 8
            for i in range(j + 1, 8):
                w[i] = a[i][j] * r
            for i in range(j + 1, 8):
                for m in range(j + 1, i + 1):
                    a[i][m] = a[i][m] - w[i] * a[m][j]
            unit = jnp.where(sub > j, c[j] * r, 0.0)
            for m in range(j + 1, 8):
                c[m] = c[m] - c[j] * w[m]
            pivot = jnp.broadcast_to(row[j : j + 1, :], (8, 256))
            row = row - jnp.concatenate([unit, unit], axis=1) * pivot
            if not last:
                lead = n[j] * r
                for m in range(j + 1, 8):
                    n[m] = n[m] - n[j] * w[m]
                below = below - jnp.concatenate([lead, lead], axis=1) * pivot
        done = row * jnp.concatenate([scale, scale], axis=1)
        u_ref[lo : lo + 8, :] = done
        before = done
        if not last:
            row = below


def gather_kernel(x_hbm, y_hbm, t_out, f_out, y_out, a_out, head, tile, other, hold, t_ref, s_ref, u_ref, sems, tree_recv, z_recv, h_recv, d_recv, t_recv, t_send, r_send, l_send, d_send, c_send, tree_send, root_send, z_send, pair_send, pair_recv):
    s = lax.axis_index("srow")
    z = lax.axis_index("scol")
    core = s % 2
    node = s // 2
    x = node % 4
    y = node // 4
    is_root = node == 0
    is_first = jnp.logical_and(s == 0, z == 0)

    def at(px, py, pcore, pz):
        return (((py % 4) * 4 + px % 4) * 2 + pcore, pz)

    def remote(src, dst, send, recv, device):
        return pltpu.make_async_remote_copy(src_ref=src, dst_ref=dst, send_sem=send, recv_sem=recv, device_id=device, device_id_type=MESH)

    mate = at(x, y, 1 - core, z)
    barrier = pltpu.get_barrier_semaphore()

    def greet_plane(j, carry):
        pl.semaphore_signal(barrier, inc=1, device_id=((s + j) % 32, z), device_id_type=MESH)
        return carry

    def greet_line(j, carry):
        pl.semaphore_signal(barrier, inc=1, device_id=(s, (z + j) % 8), device_id_type=MESH)
        return carry

    lax.fori_loop(1, 32, greet_plane, 0)
    lax.fori_loop(1, 8, greet_line, 0)

    @pl.when(z == 0)
    def _():
        fetch = pltpu.make_async_copy(x_hbm.at[:, 0:8, :], head, sems.at[0])
        fetch.start()
        fetch.wait()
        for q in range(4):
            tile[:, 128 * q : 128 * q + 128] = head[:, q, :]

    pieces = []
    for k in range(4):
        if k:
            pieces.append((k, 0, 128 * k))
        pieces.append((k, 128 * k, 128))

    def piece_rows(k, q):
        return pl.ds(pl.multiple_of(128 * k + 32 * q, 32), 32)

    def lanes(p, shift=0):
        return slice(pieces[p][1] + shift, pieces[p][1] + pieces[p][2] + shift)

    def feed(begin, end):
        def send(n, carry):
            for t in range(4):
                target = at(STEPS[t][0] + 4, STEPS[t][1] + 4, 1, z)

                @pl.when(n < 16)
                def _():
                    block = pl.ds(128 * t + 8 * n, 8)
                    remote(x_hbm.at[block], f_out.at[block], root_send.at[t], tree_recv.at[t, n], target).start()

                @pl.when(n >= 16)
                def _():
                    block = pl.ds(pl.multiple_of(128 * t + 16 * (n - 16), 16), 16)
                    remote(y_hbm.at[block], y_out.at[block], root_send.at[t + 4], tree_recv.at[t, n], target).start()

            return carry

        lax.fori_loop(begin, end, send, 0)

    def hand_over():
        remote(x_hbm, f_out, pair_send.at[0], pair_recv.at[0], mate).start()
        remote(y_hbm, y_out, pair_send.at[1], pair_recv.at[1], mate).start()

    def give_tile():
        remote(tile, other, sems.at[1], sems.at[2], mate).start()
        pltpu.make_async_copy(tile, a_out, sems.at[3]).start()

    @pl.when(is_first)
    def _():
        t_ref[:, 0:512] = tile[...]
        t_ref[:, 512:1024] = jnp.zeros((512, 512), F32)
        rows = lax.broadcasted_iota(jnp.int32, (128, 128), 0)
        cols = lax.broadcasted_iota(jnp.int32, (128, 128), 1)

        def give(p):
            k = pieces[p][0]
            for q, (dx, dy) in enumerate(STEPS):
                remote(t_ref.at[128 * k + 32 * q : 128 * k + 32 * q + 32, lanes(p, 512)], hold.at[k, :, lanes(p)], r_send.at[p], h_recv.at[p], at(dx + 4, dy + 4, 0, 0)).start()

        def given(p):
            part = t_ref.at[0:128, lanes(p, 512)]
            remote(part, part, r_send.at[p], h_recv.at[p], mate).wait_send()

        def step(k, carry):
            base = pl.multiple_of(k * 128, 128)
            mine = pl.ds(base, 128)
            s_ref[:, 0:128] = t_ref[mine, mine]
            s_ref[:, 128:256] = (rows == cols).astype(F32)
            factor_block(s_ref, u_ref)
            inverse = u_ref[:, 128:256]
            t_ref[mine, mine] = jnp.where(rows <= cols, u_ref[:, 0:128], 0.0)
            t_ref[mine, pl.ds(pl.multiple_of(base + 512, 128), 128)] = inverse

            @pl.when(k == 0)
            def _():
                pl.semaphore_wait(barrier, 38)

            for j in range(4):

                @pl.when(k == j)
                def _():
                    give(2 * j)
                    if j:
                        given(2 * j - 1)

            @pl.when(k == 0)
            def _():
                give_tile()
                feed(0, 9)

            @pl.when(k == 1)
            def _():
                feed(9, 18)

            @pl.when(k == 2)
            def _():
                feed(18, CHUNKS)
                hand_over()

            middle = pl.ds(pl.multiple_of(base + 128, 128), 384)
            t_ref[mine, middle] = jnp.dot(inverse, t_ref[mine, middle], precision=HIGHEST, preferred_element_type=F32)

            @pl.when(k < 3)
            def _():
                later = pl.multiple_of(base + 128, 128)
                coming = pl.ds(later, 128)
                window = pl.ds(later, 640)

                def take(m, inner):
                    above = pl.ds(pl.multiple_of(m * 128, 128), 128)
                    t_ref[coming, window] = t_ref[coming, window] - tdot(t_ref[above, coming], t_ref[above, window])
                    return inner

                lax.fori_loop(0, k + 1, take, 0)

            for j in range(3):

                @pl.when(k == j)
                def _():
                    give(2 * j + 1)

            return carry

        lax.fori_loop(0, 4, step, 0)
        keep = pltpu.make_async_copy(t_ref.at[:, 0:512], t_out.at[:, 0:512], sems.at[0])
        keep.start()
        for j in range(4):
            given(2 * j)
        keep.wait()

    @pl.when(jnp.logical_not(is_first))
    def _():
        pl.semaphore_wait(barrier, 38)

        @pl.when(z == 0)
        def _():
            give_tile()

        @pl.when(s == 0)
        def _():
            feed(0, CHUNKS)
            hand_over()

    @pl.when(core == 0)
    def _():
        quarter = jnp.where(x == 1, 0, jnp.where(y == 1, 1, jnp.where(x == 3, 2, 3)))
        holder = jnp.logical_or(jnp.logical_and(y == 0, x % 2 == 1), jnp.logical_and(x == 0, y % 2 == 1))

        @pl.when(holder)
        def _():
            for p, (k, _, _) in enumerate(pieces):
                part = hold.at[k, :, lanes(p)]
                mine = t_out.at[piece_rows(k, quarter), lanes(p, 512)]
                remote(part, part, r_send.at[p], h_recv.at[p], mate).wait_recv()

                @pl.when(z == 0)
                def _():
                    for far in (4, 3, 5, 2, 6, 1, 7):
                        remote(part, part, l_send.at[p], h_recv.at[p], (s, far)).start()

                def around(j, carry):
                    remote(part, mine, d_send.at[p], d_recv.at[p], ((s + 2 * j) % 32, z)).start()
                    return carry

                lax.fori_loop(1, 16, around, 0)
                pltpu.make_async_copy(part, mine, c_send.at[p]).start()

        for p, (k, _, _) in enumerate(pieces):

            @pl.when(holder)
            def _():
                part = t_out.at[0:96, lanes(p, 512)]
                remote(part, part, d_send.at[p], d_recv.at[p], mate).wait_recv()
                pltpu.make_async_copy(hold.at[k, :, lanes(p)], t_out.at[piece_rows(k, quarter), lanes(p, 512)], c_send.at[p]).wait()

            whole = t_out.at[128 * k : 128 * k + 128, lanes(p, 512)]

            @pl.when(jnp.logical_not(holder))
            def _():
                remote(whole, whole, d_send.at[p], d_recv.at[p], mate).wait_recv()

            remote(whole, whole, t_send.at[p], t_recv.at[p], mate).start()

        for p, (k, _, _) in enumerate(pieces):
            whole = t_out.at[128 * k : 128 * k + 128, lanes(p, 512)]
            remote(whole, whole, t_send.at[p], t_recv.at[p], mate).wait_send()

            @pl.when(holder)
            def _():
                part = t_ref.at[0:480, lanes(p)]
                remote(part, part, d_send.at[p], d_recv.at[p], mate).wait_send()

                @pl.when(z == 0)
                def _():
                    part = t_ref.at[0:224, lanes(p)]
                    remote(part, part, l_send.at[p], h_recv.at[p], mate).wait_send()

        @pl.when(z == 0)
        def _():
            remote(tile, other, sems.at[1], sems.at[2], mate).wait_recv()
            remote(tile, other, sems.at[1], sems.at[2], mate).wait_send()
            pltpu.make_async_copy(tile, a_out, sems.at[3]).wait()

        @pl.when(z != 0)
        def _():
            remote(a_out, a_out, pair_send.at[2], pair_recv.at[2], mate).wait_recv()

        @pl.when(is_root)
        def _():
            remote(f_out, f_out, pair_send.at[0], pair_recv.at[0], mate).wait_send()
            remote(y_out, y_out, pair_send.at[1], pair_recv.at[1], mate).wait_send()
            for t in range(4):
                f_part = f_out.at[0:128]
                y_part = y_out.at[0:128]
                remote(f_part, f_part, root_send.at[t], pair_recv.at[0], mate).wait_send()
                remote(y_part, y_part, root_send.at[t + 4], pair_recv.at[1], mate).wait_send()

        @pl.when(jnp.logical_not(is_root))
        def _():
            remote(f_out, f_out, pair_send.at[0], pair_recv.at[0], mate).wait_recv()
            remote(y_out, y_out, pair_send.at[1], pair_recv.at[1], mate).wait_recv()

    @pl.when(core == 1)
    def _():
        places = ((x, y), (y, 4 - x), (4 - x, 4 - y), (4 - y, x))
        starts = []
        gives = []
        for t in range(4):
            u = (places[t][1] % 4) * 4 + places[t][0] % 4
            depth = 0
            for n, d in enumerate(DEPTH):
                depth = depth + d * (u == n).astype(jnp.int32)
            starts.append(depth * HOP)
            mine = [None] * 4
            for d in range(4):
                hit = u == KIDS[d][0]
                for n in KIDS[d][1:]:
                    hit = jnp.logical_or(hit, u == n)
                mine[(d + t) % 4] = hit
            gives.append(mine)

        def f_copy(t, n, send, recv, device):
            block = f_out.at[pl.ds(128 * t + 8 * n, 8)]
            return remote(block, block, send, recv, device)

        def y_copy(t, n, send, recv, device):
            block = y_out.at[pl.ds(pl.multiple_of(128 * t + 16 * n, 16), 16)]
            return remote(block, block, send, recv, device)

        def neighbour(d):
            return at(x + STEPS[d][0] + 4, y + STEPS[d][1] + 4, 1, z)

        z_depth = jnp.minimum(z, 8 - z)
        z_up = z < 4
        z_down = jnp.logical_or(z == 0, z > 5)

        def z_step(i):
            for k in range(2):

                @pl.when(i % 2 == k)
                def _():
                    rows = pl.ds(pl.multiple_of(32 * (i // 2), 32), 32)
                    dst = a_out if k == 0 else other

                    def send(src):
                        @pl.when(z_up)
                        def _():
                            remote(src.at[rows], dst.at[rows], z_send.at[k], z_recv.at[i], (s, (z + 1) % 8)).start()

                        @pl.when(z_down)
                        def _():
                            remote(src.at[rows], dst.at[rows], z_send.at[k + 2], z_recv.at[i], (s, (z + 7) % 8)).start()

                    @pl.when(z == 0)
                    def _():
                        send(tile if k == 0 else other)

                    @pl.when(z != 0)
                    def _():
                        remote(dst.at[rows], dst.at[rows], z_send.at[k], z_recv.at[i], mate).wait_recv()
                        send(dst)
                        if k == 1:
                            remote(other.at[rows], a_out.at[rows], pair_send.at[2], pair_recv.at[2], mate).start()

        def flow(kind, t, n, copy):
            copy(t, n, tree_send.at[kind, 0], tree_recv.at[t, n + 16 * kind], mate).wait_recv()
            for d in range(4):

                @pl.when(gives[t][d])
                def _():
                    copy(t, n, tree_send.at[kind, 4 * t + d], tree_recv.at[t, n + 16 * kind], neighbour(d)).start()

            copy(t, n, pair_send.at[kind], pair_recv.at[kind], mate).start()

        def slot(i, carry):
            for t in range(4):
                n = jnp.where(is_root, -1, i - starts[t])

                @pl.when(jnp.logical_and(n >= 0, n < 16))
                def _():
                    flow(0, t, n, f_copy)

                @pl.when(jnp.logical_and(n >= 16, n < CHUNKS))
                def _():
                    flow(1, t, n - 16, y_copy)

            zi = i - HOP * z_depth - 4

            @pl.when(jnp.logical_and(z == 0, zi == 0))
            def _():
                remote(tile, other, sems.at[1], sems.at[2], mate).wait_recv()

            @pl.when(jnp.logical_and(zi >= 0, zi < 32))
            def _():
                z_step(zi)

            return carry

        lax.fori_loop(0, 36 + 4 * HOP, slot, 0)

        f_part = f_out.at[0:128]
        y_part = y_out.at[0:128]

        @pl.when(is_root)
        def _():
            remote(f_out, f_out, pair_send.at[0], pair_recv.at[0], mate).wait_recv()
            remote(y_out, y_out, pair_send.at[1], pair_recv.at[1], mate).wait_recv()

        @pl.when(jnp.logical_not(is_root))
        def _():
            for t in range(4):
                for d in range(4):

                    @pl.when(gives[t][d])
                    def _():
                        remote(f_part, f_part, tree_send.at[0, 4 * t + d], pair_recv.at[0], mate).wait_send()
                        remote(y_part, y_part, tree_send.at[1, 4 * t + d], pair_recv.at[1], mate).wait_send()

            remote(f_out, f_out, pair_send.at[0], pair_recv.at[0], mate).wait_send()
            remote(y_out, y_out, pair_send.at[1], pair_recv.at[1], mate).wait_send()

        for k in range(2):

            @pl.when(z_up)
            def _():
                remote(a_out, a_out, z_send.at[k], pair_recv.at[2], mate).wait_send()

            @pl.when(z_down)
            def _():
                remote(a_out, a_out, z_send.at[k + 2], pair_recv.at[2], mate).wait_send()

        @pl.when(z == 0)
        def _():
            remote(tile, other, sems.at[1], sems.at[2], mate).wait_send()
            pltpu.make_async_copy(tile, a_out, sems.at[3]).wait()

        @pl.when(z != 0)
        def _():
            remote(a_out, a_out, pair_send.at[2], pair_recv.at[2], mate).wait_send()

        for p, (k, _, _) in enumerate(pieces):
            whole = t_out.at[128 * k : 128 * k + 128, lanes(p, 512)]
            remote(whole, whole, t_send.at[p], t_recv.at[p], mate).wait_recv()


def gather(x, y):
    dma = pltpu.SemaphoreType.DMA
    anyspace = pl.BlockSpec(memory_space=pl.ANY)
    return pl.pallas_call(
        gather_kernel,
        out_shape=(
            jax.ShapeDtypeStruct((512, 1024), F32),
            jax.ShapeDtypeStruct((512, 16, 128), F32),
            jax.ShapeDtypeStruct((512, 1024), F32),
            jax.ShapeDtypeStruct((512, 512), F32),
        ),
        in_specs=[pl.BlockSpec(memory_space=pltpu.HBM)] * 2,
        out_specs=[anyspace] * 4,
        scratch_shapes=[
            pltpu.VMEM((512, 8, 128), F32),
            pltpu.VMEM((512, 512), F32),
            pltpu.VMEM((512, 512), F32),
            pltpu.VMEM((4, 32, 512), F32),
            pltpu.VMEM((512, 1024), F32),
            pltpu.VMEM((128, 256), F32),
            pltpu.VMEM((128, 256), F32),
            dma((4,)),
            dma((4, CHUNKS)),
            dma((32,)),
            dma((7,)),
            dma((7,)),
            dma((7,)),
            dma((7,)),
            dma((7,)),
            dma((7,)),
            dma((7,)),
            dma((7,)),
            dma((2, 16)),
            dma((8,)),
            dma((4,)),
            dma((3,)),
            dma((3,)),
        ],
        compiler_params=pltpu.CompilerParams(collective_id=0, has_side_effects=True, vmem_limit_bytes=53 << 20),
        name="gather",
    )(x, y)


def split(v):
    high = v.astype(BF16)
    return high, (v - high.astype(F32)).astype(BF16)


def dot3(a, b, dims=(((1,), (0,)), ((), ()))):
    ah, al = a
    bh, bl = b
    dot = functools.partial(lax.dot_general, dimension_numbers=dims, preferred_element_type=F32)
    return dot(ah, bh) + (dot(ah, bl) + dot(al, bh))


def update_kernel(t_hbm, f_hbm, r_hbm, a_hbm, x_hbm, y_hbm, fo_hbm, yo_hbm, t, a, f, r, x, y, fo, yo, sems):
    s = lax.axis_index("srow")
    z = lax.axis_index("scol")
    loads = [
        pltpu.make_async_copy(src, dst, sems.at[i])
        for i, (src, dst) in enumerate(((t_hbm, t), (a_hbm, a), (f_hbm, f), (x_hbm, x), (r_hbm, r), (y_hbm, y)))
    ]
    stores = [pltpu.make_async_copy(src, dst, sems.at[6 + i]) for i, (src, dst) in enumerate(((fo, fo_hbm), (yo, yo_hbm)))]
    for load in loads:
        load.start()
    loads[0].wait()
    loads[1].wait()

    def lane(ref, i):
        return ref.at[pl.ds(i, 512, stride=16), :]

    def inverse_rows(k):
        rows = slice(128 * k, 128 * k + 128)
        own = t[rows, 512 + 128 * k : 640 + 128 * k]
        if k == 0:
            return own
        left = dot3(split(own), split(t[rows, 512 : 512 + 128 * k]))
        return jnp.concatenate([left, own], axis=1)

    def padded_rows(k):
        rows = inverse_rows(k)
        return rows if k == 3 else jnp.concatenate([rows, jnp.zeros((128, 384 - 128 * k), F32)], axis=1)

    @pl.when(s != 0)
    def _():
        inverse = split(jnp.concatenate([padded_rows(k) for k in range(4)], axis=0))
        panel = dot3(split(a[...]), inverse, (((1,), (1,)), ((), ())))
        q = split(dot3(split(panel), inverse))
        loads[2].wait()
        loads[3].wait()
        for c in range(4):
            right = split(jnp.concatenate([lane(f, 4 * c + j)[...] for j in range(4)], axis=1))
            change = dot3(q, right)
            for j in range(4):
                lane(fo, 4 * c + j)[...] = lane(x, 4 * c + j)[...] - change[:, 128 * j : 128 * j + 128]

        @pl.when(z == 0)
        def _():
            for j in range(4):
                lane(fo, j)[...] = panel[:, 128 * j : 128 * j + 128]

        stores[0].start()
        loads[4].wait()
        loads[5].wait()
        for c in range(2):
            part = slice(512 * c, 512 * c + 512)
            yo[:, part] = y[:, part] - dot3(q, split(r[:, part]))
        stores[1].start()

    @pl.when(s == 0)
    def _():
        fo[...] = jnp.zeros_like(fo)

        @pl.when(z == 0)
        def _():
            rows = lax.broadcasted_iota(jnp.int32, (512, 512), 0)
            cols = lax.broadcasted_iota(jnp.int32, (512, 512), 1)
            lower = jnp.where(rows >= cols, t[:, 0:512].T, 0.0)
            for j in range(4):
                lane(fo, j)[...] = lower[:, 128 * j : 128 * j + 128]

        stores[0].start()
        for load in loads[2:]:
            load.wait()
        ys = split(y[...])
        for k in range(4):
            width = 128 * k + 128
            yo[128 * k : width, :] = dot3(split(inverse_rows(k)), (ys[0][:width], ys[1][:width]))
        stores[1].start()

    stores[0].wait()
    stores[1].wait()


def update(t, f, r, a, x, y):
    anyspace = pl.BlockSpec(memory_space=pl.ANY)
    return pl.pallas_call(
        update_kernel,
        out_shape=(jax.ShapeDtypeStruct((8192, 128), F32), jax.ShapeDtypeStruct((512, 1024), F32)),
        in_specs=[anyspace] * 6,
        out_specs=[anyspace] * 2,
        scratch_shapes=[
            pltpu.VMEM((512, 1024), F32),
            pltpu.VMEM((512, 512), F32),
            pltpu.VMEM((8192, 128), F32),
            pltpu.VMEM((512, 1024), F32),
            pltpu.VMEM((8192, 128), F32),
            pltpu.VMEM((512, 1024), F32),
            pltpu.VMEM((8192, 128), F32),
            pltpu.VMEM((512, 1024), F32),
            pltpu.SemaphoreType.DMA((8,)),
        ],
        compiler_params=pltpu.CompilerParams(vmem_limit_bytes=56 << 20),
        name="update",
    )(t, f, r, a, x, y)


def per_device(factor_state, data):
    x = factor_state.reshape(512, 16, 128)
    y = data.reshape(512, 1024)
    t, f, r, a = gather(x, y)
    factor_out, data_out = update(t, f.reshape(8192, 128), r, a, x.reshape(8192, 128), y)
    return factor_out.reshape(factor_state.shape), data_out.reshape(data.shape)


def solution(mesh):
    specs = (P("srow", None, None, "scol", None), P("srow", None, "scol"))
    return jax.shard_map(per_device, mesh=mesh, in_specs=specs, out_specs=specs, check_vma=False)
```

```python
import functools

import jax
import jax.numpy as jnp
from jax import lax
from jax.experimental import pallas as pl
from jax.experimental.pallas import tpu as pltpu
from jax.sharding import PartitionSpec as P

F32 = jnp.float32
BF16 = jnp.bfloat16
HIGHEST = lax.Precision.HIGHEST
MESH = pl.DeviceIdType.MESH
STEPS = ((1, 0), (0, 1), (-1, 0), (0, -1))
DEPTH = (0, 1, 2, 3, 3, 2, 3, 4, 4, 3, 4, 5, 3, 2, 3, 4)
KIDS = ((0, 1, 2, 5, 6, 10, 14), (1, 5), (5, 9, 13), (1, 2, 14))
HOP = 3
CHUNKS = 12


def tdot(a, b):
    return lax.dot_general(a, b, (((0,), (0,)), ((), ())), precision=HIGHEST, preferred_element_type=F32)


def factor_block(s_ref, u_ref):
    sub = lax.broadcasted_iota(jnp.int32, (8, 128), 0)
    row = s_ref[0:8, :]
    before = None
    for k in range(16):
        lo = 8 * k
        last = k == 15
        if before is not None and not last:
            s_ref[lo + 8 : 128, :] = s_ref[lo + 8 : 128, :] - tdot(before[:, lo + 8 : 128], before)
        c = [jnp.broadcast_to(row[:, lo + m : lo + m + 1], (8, 128)) for m in range(8)]
        a = [[jnp.broadcast_to(c[j][i : i + 1, :], (8, 128)) if i >= j else None for j in range(8)] for i in range(8)]
        if not last:
            below = s_ref[lo + 8 : lo + 16, :]
            n = [jnp.broadcast_to(below[:, lo + m : lo + m + 1], (8, 128)) for m in range(8)]
        scale = jnp.zeros((8, 128), F32)
        for j in range(8):
            q = lax.rsqrt(a[j][j])
            r = q * q
            scale = jnp.where(sub == j, q, scale)
            w = [None] * 8
            for i in range(j + 1, 8):
                w[i] = a[i][j] * r
            for i in range(j + 1, 8):
                for m in range(j + 1, i + 1):
                    a[i][m] = a[i][m] - w[i] * a[m][j]
            unit = jnp.where(sub > j, c[j] * r, 0.0)
            for m in range(j + 1, 8):
                c[m] = c[m] - c[j] * w[m]
            pivot = jnp.broadcast_to(row[j : j + 1, :], (8, 256))
            row = row - jnp.concatenate([unit, unit], axis=1) * pivot
            if not last:
                lead = n[j] * r
                for m in range(j + 1, 8):
                    n[m] = n[m] - n[j] * w[m]
                below = below - jnp.concatenate([lead, lead], axis=1) * pivot
        done = row * jnp.concatenate([scale, scale], axis=1)
        u_ref[lo : lo + 8, :] = done
        before = done
        if not last:
            row = below


def gather_kernel(x_hbm, y_hbm, t_out, f_out, y_out, a_out, head, tile, other, hold, t_ref, s_ref, u_ref, sems, tree_recv, z_recv, h_recv, d_recv, t_recv, t_send, r_send, l_send, d_send, c_send, tree_send, root_send, z_send, pair_send, pair_recv):
    s = lax.axis_index("srow")
    z = lax.axis_index("scol")
    core = s % 2
    node = s // 2
    x = node % 4
    y = node // 4
    is_root = node == 0
    is_first = jnp.logical_and(s == 0, z == 0)

    def at(px, py, pcore, pz):
        return (((py % 4) * 4 + px % 4) * 2 + pcore, pz)

    def remote(src, dst, send, recv, device):
        return pltpu.make_async_remote_copy(src_ref=src, dst_ref=dst, send_sem=send, recv_sem=recv, device_id=device, device_id_type=MESH)

    mate = at(x, y, 1 - core, z)
    barrier = pltpu.get_barrier_semaphore()

    def greet_plane(j, carry):
        pl.semaphore_signal(barrier, inc=1, device_id=((s + j) % 32, z), device_id_type=MESH)
        return carry

    def greet_line(j, carry):
        pl.semaphore_signal(barrier, inc=1, device_id=(s, (z + j) % 8), device_id_type=MESH)
        return carry

    lax.fori_loop(1, 32, greet_plane, 0)
    lax.fori_loop(1, 8, greet_line, 0)

    @pl.when(z == 0)
    def _():
        fetch = pltpu.make_async_copy(x_hbm.at[:, 0:8, :], head, sems.at[0])
        fetch.start()
        fetch.wait()
        for q in range(4):
            tile[:, 128 * q : 128 * q + 128] = head[:, q, :]

    pieces = []
    for k in range(4):
        if k:
            pieces.append((k, 0, 128 * k))
        pieces.append((k, 128 * k, 128))

    def piece_rows(k, q):
        return pl.ds(pl.multiple_of(128 * k + 32 * q, 32), 32)

    def lanes(p, shift=0):
        return slice(pieces[p][1] + shift, pieces[p][1] + pieces[p][2] + shift)

    def feed(begin, end):
        def send(n, carry):
            for t in range(4):
                target = at(STEPS[t][0] + 4, STEPS[t][1] + 4, 1, z)

                @pl.when(n < 8)
                def _():
                    block = pl.ds(128 * t + 16 * n, 16)
                    remote(x_hbm.at[block], f_out.at[block], root_send.at[t], tree_recv.at[t, n], target).start()

                @pl.when(n >= 8)
                def _():
                    block = pl.ds(pl.multiple_of(128 * t + 32 * (n - 8), 32), 32)
                    remote(y_hbm.at[block], y_out.at[block], root_send.at[t + 4], tree_recv.at[t, n], target).start()

            return carry

        lax.fori_loop(begin, end, send, 0)

    def hand_over():
        remote(x_hbm, f_out, pair_send.at[0], pair_recv.at[0], mate).start()
        remote(y_hbm, y_out, pair_send.at[1], pair_recv.at[1], mate).start()

    def give_tile():
        remote(tile, other, sems.at[1], sems.at[2], mate).start()
        pltpu.make_async_copy(tile, a_out, sems.at[3]).start()

    @pl.when(is_first)
    def _():
        t_ref[:, 0:512] = tile[...]
        t_ref[:, 512:1024] = jnp.zeros((512, 512), F32)
        rows = lax.broadcasted_iota(jnp.int32, (128, 128), 0)
        cols = lax.broadcasted_iota(jnp.int32, (128, 128), 1)

        def give(p):
            k = pieces[p][0]
            for q, (dx, dy) in enumerate(STEPS):
                remote(t_ref.at[128 * k + 32 * q : 128 * k + 32 * q + 32, lanes(p, 512)], hold.at[k, :, lanes(p)], r_send.at[p], h_recv.at[p], at(dx + 4, dy + 4, 0, 0)).start()

        def given(p):
            part = t_ref.at[0:128, lanes(p, 512)]
            remote(part, part, r_send.at[p], h_recv.at[p], mate).wait_send()

        def step(k, carry):
            base = pl.multiple_of(k * 128, 128)
            mine = pl.ds(base, 128)
            s_ref[:, 0:128] = t_ref[mine, mine]
            s_ref[:, 128:256] = (rows == cols).astype(F32)
            factor_block(s_ref, u_ref)
            inverse = u_ref[:, 128:256]
            t_ref[mine, mine] = jnp.where(rows <= cols, u_ref[:, 0:128], 0.0)
            t_ref[mine, pl.ds(pl.multiple_of(base + 512, 128), 128)] = inverse

            @pl.when(k == 0)
            def _():
                pl.semaphore_wait(barrier, 38)

            for j in range(4):

                @pl.when(k == j)
                def _():
                    give(2 * j)
                    if j:
                        given(2 * j - 1)

            @pl.when(k == 0)
            def _():
                give_tile()
                feed(0, 5)

            @pl.when(k == 1)
            def _():
                feed(5, 9)

            @pl.when(k == 2)
            def _():
                feed(9, CHUNKS)
                hand_over()

            middle = pl.ds(pl.multiple_of(base + 128, 128), 384)
            t_ref[mine, middle] = jnp.dot(inverse, t_ref[mine, middle], precision=HIGHEST, preferred_element_type=F32)

            @pl.when(k < 3)
            def _():
                later = pl.multiple_of(base + 128, 128)
                coming = pl.ds(later, 128)
                window = pl.ds(later, 640)

                def take(m, inner):
                    above = pl.ds(pl.multiple_of(m * 128, 128), 128)
                    t_ref[coming, window] = t_ref[coming, window] - tdot(t_ref[above, coming], t_ref[above, window])
                    return inner

                lax.fori_loop(0, k + 1, take, 0)

            for j in range(3):

                @pl.when(k == j)
                def _():
                    give(2 * j + 1)

            return carry

        lax.fori_loop(0, 4, step, 0)
        keep = pltpu.make_async_copy(t_ref.at[:, 0:512], t_out.at[:, 0:512], sems.at[0])
        keep.start()
        for j in range(4):
            given(2 * j)
        keep.wait()

    @pl.when(jnp.logical_not(is_first))
    def _():
        pl.semaphore_wait(barrier, 38)

        @pl.when(z == 0)
        def _():
            give_tile()

        @pl.when(s == 0)
        def _():
            feed(0, CHUNKS)
            hand_over()

    @pl.when(core == 0)
    def _():
        quarter = jnp.where(x == 1, 0, jnp.where(y == 1, 1, jnp.where(x == 3, 2, 3)))
        holder = jnp.logical_or(jnp.logical_and(y == 0, x % 2 == 1), jnp.logical_and(x == 0, y % 2 == 1))

        @pl.when(holder)
        def _():
            for p, (k, _, _) in enumerate(pieces):
                part = hold.at[k, :, lanes(p)]
                mine = t_out.at[piece_rows(k, quarter), lanes(p, 512)]
                remote(part, part, r_send.at[p], h_recv.at[p], mate).wait_recv()

                @pl.when(z == 0)
                def _():
                    for far in (4, 3, 5, 2, 6, 1, 7):
                        remote(part, part, l_send.at[p], h_recv.at[p], (s, far)).start()

                def around(j, carry):
                    remote(part, mine, d_send.at[p], d_recv.at[p], ((s + 2 * j) % 32, z)).start()
                    return carry

                lax.fori_loop(1, 16, around, 0)
                pltpu.make_async_copy(part, mine, c_send.at[p]).start()

        for p, (k, _, _) in enumerate(pieces):

            @pl.when(holder)
            def _():
                part = t_out.at[0:96, lanes(p, 512)]
                remote(part, part, d_send.at[p], d_recv.at[p], mate).wait_recv()
                pltpu.make_async_copy(hold.at[k, :, lanes(p)], t_out.at[piece_rows(k, quarter), lanes(p, 512)], c_send.at[p]).wait()

            whole = t_out.at[128 * k : 128 * k + 128, lanes(p, 512)]

            @pl.when(jnp.logical_not(holder))
            def _():
                remote(whole, whole, d_send.at[p], d_recv.at[p], mate).wait_recv()

            remote(whole, whole, t_send.at[p], t_recv.at[p], mate).start()

        for p, (k, _, _) in enumerate(pieces):
            whole = t_out.at[128 * k : 128 * k + 128, lanes(p, 512)]
            remote(whole, whole, t_send.at[p], t_recv.at[p], mate).wait_send()

            @pl.when(holder)
            def _():
                part = t_ref.at[0:480, lanes(p)]
                remote(part, part, d_send.at[p], d_recv.at[p], mate).wait_send()

                @pl.when(z == 0)
                def _():
                    part = t_ref.at[0:224, lanes(p)]
                    remote(part, part, l_send.at[p], h_recv.at[p], mate).wait_send()

        @pl.when(z == 0)
        def _():
            remote(tile, other, sems.at[1], sems.at[2], mate).wait_recv()
            remote(tile, other, sems.at[1], sems.at[2], mate).wait_send()
            pltpu.make_async_copy(tile, a_out, sems.at[3]).wait()

        @pl.when(z != 0)
        def _():
            remote(a_out, a_out, pair_send.at[2], pair_recv.at[2], mate).wait_recv()

        @pl.when(is_root)
        def _():
            remote(f_out, f_out, pair_send.at[0], pair_recv.at[0], mate).wait_send()
            remote(y_out, y_out, pair_send.at[1], pair_recv.at[1], mate).wait_send()
            for t in range(4):
                f_part = f_out.at[0:128]
                y_part = y_out.at[0:128]
                remote(f_part, f_part, root_send.at[t], pair_recv.at[0], mate).wait_send()
                remote(y_part, y_part, root_send.at[t + 4], pair_recv.at[1], mate).wait_send()

        @pl.when(jnp.logical_not(is_root))
        def _():
            remote(f_out, f_out, pair_send.at[0], pair_recv.at[0], mate).wait_recv()
            remote(y_out, y_out, pair_send.at[1], pair_recv.at[1], mate).wait_recv()

    @pl.when(core == 1)
    def _():
        places = ((x, y), (y, 4 - x), (4 - x, 4 - y), (4 - y, x))
        starts = []
        gives = []
        for t in range(4):
            u = (places[t][1] % 4) * 4 + places[t][0] % 4
            depth = 0
            for n, d in enumerate(DEPTH):
                depth = depth + d * (u == n).astype(jnp.int32)
            starts.append(depth * HOP)
            mine = [None] * 4
            for d in range(4):
                hit = u == KIDS[d][0]
                for n in KIDS[d][1:]:
                    hit = jnp.logical_or(hit, u == n)
                mine[(d + t) % 4] = hit
            gives.append(mine)

        def f_copy(t, n, send, recv, device):
            block = f_out.at[pl.ds(128 * t + 16 * n, 16)]
            return remote(block, block, send, recv, device)

        def y_copy(t, n, send, recv, device):
            block = y_out.at[pl.ds(pl.multiple_of(128 * t + 32 * n, 32), 32)]
            return remote(block, block, send, recv, device)

        def neighbour(d):
            return at(x + STEPS[d][0] + 4, y + STEPS[d][1] + 4, 1, z)

        z_depth = jnp.minimum(z, 8 - z)
        z_up = z < 4
        z_down = jnp.logical_or(z == 0, z > 5)

        def z_step(i):
            for k in range(2):

                @pl.when(i % 2 == k)
                def _():
                    rows = pl.ds(pl.multiple_of(64 * (i // 2), 64), 64)
                    dst = a_out if k == 0 else other

                    def send(src):
                        @pl.when(z_up)
                        def _():
                            remote(src.at[rows], dst.at[rows], z_send.at[k], z_recv.at[i], (s, (z + 1) % 8)).start()

                        @pl.when(z_down)
                        def _():
                            remote(src.at[rows], dst.at[rows], z_send.at[k + 2], z_recv.at[i], (s, (z + 7) % 8)).start()

                    @pl.when(z == 0)
                    def _():
                        send(tile if k == 0 else other)

                    @pl.when(z != 0)
                    def _():
                        remote(dst.at[rows], dst.at[rows], z_send.at[k], z_recv.at[i], mate).wait_recv()
                        send(dst)
                        if k == 1:
                            remote(other.at[rows], a_out.at[rows], pair_send.at[2], pair_recv.at[2], mate).start()

        def flow(kind, t, n, copy):
            copy(t, n, tree_send.at[kind, 0], tree_recv.at[t, n + 8 * kind], mate).wait_recv()
            for d in range(4):

                @pl.when(gives[t][d])
                def _():
                    copy(t, n, tree_send.at[kind, 4 * t + d], tree_recv.at[t, n + 8 * kind], neighbour(d)).start()

            copy(t, n, pair_send.at[kind], pair_recv.at[kind], mate).start()

        def slot(i, carry):
            for t in range(4):
                n = jnp.where(is_root, -1, i - starts[t])

                @pl.when(jnp.logical_and(n >= 0, n < 8))
                def _():
                    flow(0, t, n, f_copy)

                @pl.when(jnp.logical_and(n >= 8, n < CHUNKS))
                def _():
                    flow(1, t, n - 8, y_copy)

            zi = i - HOP * z_depth - 2

            @pl.when(jnp.logical_and(z == 0, zi == 0))
            def _():
                remote(tile, other, sems.at[1], sems.at[2], mate).wait_recv()

            @pl.when(jnp.logical_and(zi >= 0, zi < 16))
            def _():
                z_step(zi)

            return carry

        lax.fori_loop(0, 18 + 5 * HOP, slot, 0)

        f_part = f_out.at[0:128]
        y_part = y_out.at[0:128]

        @pl.when(is_root)
        def _():
            remote(f_out, f_out, pair_send.at[0], pair_recv.at[0], mate).wait_recv()
            remote(y_out, y_out, pair_send.at[1], pair_recv.at[1], mate).wait_recv()

        @pl.when(jnp.logical_not(is_root))
        def _():
            for t in range(4):
                for d in range(4):

                    @pl.when(gives[t][d])
                    def _():
                        remote(f_part, f_part, tree_send.at[0, 4 * t + d], pair_recv.at[0], mate).wait_send()
                        remote(y_part, y_part, tree_send.at[1, 4 * t + d], pair_recv.at[1], mate).wait_send()

            remote(f_out, f_out, pair_send.at[0], pair_recv.at[0], mate).wait_send()
            remote(y_out, y_out, pair_send.at[1], pair_recv.at[1], mate).wait_send()

        for k in range(2):

            @pl.when(z_up)
            def _():
                remote(a_out, a_out, z_send.at[k], pair_recv.at[2], mate).wait_send()

            @pl.when(z_down)
            def _():
                remote(a_out, a_out, z_send.at[k + 2], pair_recv.at[2], mate).wait_send()

        @pl.when(z == 0)
        def _():
            remote(tile, other, sems.at[1], sems.at[2], mate).wait_send()
            pltpu.make_async_copy(tile, a_out, sems.at[3]).wait()

        @pl.when(z != 0)
        def _():
            remote(a_out, a_out, pair_send.at[2], pair_recv.at[2], mate).wait_send()

        for p, (k, _, _) in enumerate(pieces):
            whole = t_out.at[128 * k : 128 * k + 128, lanes(p, 512)]
            remote(whole, whole, t_send.at[p], t_recv.at[p], mate).wait_recv()


def gather(x, y):
    dma = pltpu.SemaphoreType.DMA
    anyspace = pl.BlockSpec(memory_space=pl.ANY)
    return pl.pallas_call(
        gather_kernel,
        out_shape=(
            jax.ShapeDtypeStruct((512, 1024), F32),
            jax.ShapeDtypeStruct((512, 16, 128), F32),
            jax.ShapeDtypeStruct((512, 1024), F32),
            jax.ShapeDtypeStruct((512, 512), F32),
        ),
        in_specs=[pl.BlockSpec(memory_space=pltpu.HBM)] * 2,
        out_specs=[anyspace] * 4,
        scratch_shapes=[
            pltpu.VMEM((512, 8, 128), F32),
            pltpu.VMEM((512, 512), F32),
            pltpu.VMEM((512, 512), F32),
            pltpu.VMEM((4, 32, 512), F32),
            pltpu.VMEM((512, 1024), F32),
            pltpu.VMEM((128, 256), F32),
            pltpu.VMEM((128, 256), F32),
            dma((4,)),
            dma((4, CHUNKS)),
            dma((16,)),
            dma((7,)),
            dma((7,)),
            dma((7,)),
            dma((7,)),
            dma((7,)),
            dma((7,)),
            dma((7,)),
            dma((7,)),
            dma((2, 16)),
            dma((8,)),
            dma((4,)),
            dma((3,)),
            dma((3,)),
        ],
        compiler_params=pltpu.CompilerParams(collective_id=0, has_side_effects=True, vmem_limit_bytes=53 << 20),
        name="gather",
    )(x, y)


def split(v):
    high = v.astype(BF16)
    return high, (v - high.astype(F32)).astype(BF16)


def dot3(a, b, dims=(((1,), (0,)), ((), ()))):
    ah, al = a
    bh, bl = b
    dot = functools.partial(lax.dot_general, dimension_numbers=dims, preferred_element_type=F32)
    return dot(ah, bh) + (dot(ah, bl) + dot(al, bh))


def update_kernel(t_hbm, f_hbm, r_hbm, a_hbm, x_hbm, y_hbm, fo_hbm, yo_hbm, t, a, f, r, x, y, fo, yo, sems):
    s = lax.axis_index("srow")
    z = lax.axis_index("scol")
    loads = [
        pltpu.make_async_copy(src, dst, sems.at[i])
        for i, (src, dst) in enumerate(((t_hbm.at[:, 512:1024], t.at[:, 512:1024]), (a_hbm, a), (f_hbm, f), (x_hbm, x), (r_hbm, r), (y_hbm, y)))
    ]
    halves = (slice(0, 512), slice(512, 1024))
    stores = [pltpu.make_async_copy(fo, fo_hbm, sems.at[6])]
    stores += [pltpu.make_async_copy(yo.at[:, half], yo_hbm.at[:, half], sems.at[7 + i]) for i, half in enumerate(halves)]
    loads[0].start()
    loads[1].start()
    loads[0].wait()
    loads[1].wait()
    for load in loads[2:]:
        load.start()

    def lane(ref, i):
        return ref.at[pl.ds(i, 512, stride=16), :]

    def inverse_rows(k):
        rows = slice(128 * k, 128 * k + 128)
        own = t[rows, 512 + 128 * k : 640 + 128 * k]
        if k == 0:
            return own
        left = dot3(split(own), split(t[rows, 512 : 512 + 128 * k]))
        return jnp.concatenate([left, own], axis=1)

    def padded_rows(k):
        rows = inverse_rows(k)
        return rows if k == 3 else jnp.concatenate([rows, jnp.zeros((128, 384 - 128 * k), F32)], axis=1)

    @pl.when(s != 0)
    def _():
        inverse = split(jnp.concatenate([padded_rows(k) for k in range(4)], axis=0))
        panel = dot3(split(a[...]), inverse, (((1,), (1,)), ((), ())))
        q = split(dot3(split(panel), inverse))
        loads[2].wait()
        loads[3].wait()
        for c in range(4):
            right = split(jnp.concatenate([lane(f, 4 * c + j)[...] for j in range(4)], axis=1))
            change = dot3(q, right)
            for j in range(4):
                lane(fo, 4 * c + j)[...] = lane(x, 4 * c + j)[...] - change[:, 128 * j : 128 * j + 128]

        @pl.when(z == 0)
        def _():
            for j in range(4):
                lane(fo, j)[...] = panel[:, 128 * j : 128 * j + 128]

        stores[0].start()
        loads[4].wait()
        loads[5].wait()
        for c, part in enumerate(halves):
            yo[:, part] = y[:, part] - dot3(q, split(r[:, part]))
            stores[1 + c].start()

    @pl.when(s == 0)
    def _():
        fo[...] = jnp.zeros_like(fo)

        @pl.when(z == 0)
        def _():
            upper = pltpu.make_async_copy(t_hbm.at[:, 0:512], t.at[:, 0:512], sems.at[0])
            upper.start()
            upper.wait()
            rows = lax.broadcasted_iota(jnp.int32, (512, 512), 0)
            cols = lax.broadcasted_iota(jnp.int32, (512, 512), 1)
            lower = jnp.where(rows >= cols, t[:, 0:512].T, 0.0)
            for j in range(4):
                lane(fo, j)[...] = lower[:, 128 * j : 128 * j + 128]

        stores[0].start()
        for load in loads[2:]:
            load.wait()
        ys = split(y[...])
        for k in range(4):
            width = 128 * k + 128
            yo[128 * k : width, :] = dot3(split(inverse_rows(k)), (ys[0][:width], ys[1][:width]))
        stores[1].start()
        stores[2].start()

    for store in stores:
        store.wait()


def update(t, f, r, a, x, y):
    anyspace = pl.BlockSpec(memory_space=pl.ANY)
    return pl.pallas_call(
        update_kernel,
        out_shape=(jax.ShapeDtypeStruct((8192, 128), F32), jax.ShapeDtypeStruct((512, 1024), F32)),
        in_specs=[anyspace] * 6,
        out_specs=[anyspace] * 2,
        scratch_shapes=[
            pltpu.VMEM((512, 1024), F32),
            pltpu.VMEM((512, 512), F32),
            pltpu.VMEM((8192, 128), F32),
            pltpu.VMEM((512, 1024), F32),
            pltpu.VMEM((8192, 128), F32),
            pltpu.VMEM((512, 1024), F32),
            pltpu.VMEM((8192, 128), F32),
            pltpu.VMEM((512, 1024), F32),
            pltpu.SemaphoreType.DMA((9,)),
        ],
        compiler_params=pltpu.CompilerParams(vmem_limit_bytes=56 << 20),
        name="update",
    )(t, f, r, a, x, y)


def per_device(factor_state, data):
    x = factor_state.reshape(512, 16, 128)
    y = data.reshape(512, 1024)
    t, f, r, a = gather(x, y)
    factor_out, data_out = update(t, f.reshape(8192, 128), r, a, x.reshape(8192, 128), y)
    return factor_out.reshape(factor_state.shape), data_out.reshape(data.shape)


def solution(mesh):
    specs = (P("srow", None, None, "scol", None), P("srow", None, "scol"))
    return jax.shard_map(per_device, mesh=mesh, in_specs=specs, out_specs=specs, check_vma=False)
```

```python
import functools

import jax
import jax.numpy as jnp
from jax import lax
from jax.experimental import pallas as pl
from jax.experimental.pallas import tpu as pltpu
from jax.sharding import PartitionSpec as P

F32 = jnp.float32
BF16 = jnp.bfloat16
HIGHEST = lax.Precision.HIGHEST
MESH = pl.DeviceIdType.MESH
STEPS = ((1, 0), (0, 1), (-1, 0), (0, -1))
DEPTH = (0, 1, 2, 3, 3, 2, 3, 4, 4, 3, 4, 5, 3, 2, 3, 4)
KIDS = ((0, 1, 2, 5, 6, 10, 14), (1, 5), (5, 9, 13), (1, 2, 14))
HOP = 4
CHUNKS = 24


def tdot(a, b):
    return lax.dot_general(a, b, (((0,), (0,)), ((), ())), precision=HIGHEST, preferred_element_type=F32)


def factor_block(s_ref, u_ref):
    sub = lax.broadcasted_iota(jnp.int32, (8, 128), 0)
    row = s_ref[0:8, :]
    before = None
    for k in range(16):
        lo = 8 * k
        last = k == 15
        if before is not None and not last:
            s_ref[lo + 8 : 128, :] = s_ref[lo + 8 : 128, :] - tdot(before[:, lo + 8 : 128], before)
        c = [jnp.broadcast_to(row[:, lo + m : lo + m + 1], (8, 128)) for m in range(8)]
        a = [[jnp.broadcast_to(c[j][i : i + 1, :], (8, 128)) if i >= j else None for j in range(8)] for i in range(8)]
        if not last:
            below = s_ref[lo + 8 : lo + 16, :]
            n = [jnp.broadcast_to(below[:, lo + m : lo + m + 1], (8, 128)) for m in range(8)]
        scale = jnp.zeros((8, 128), F32)
        for j in range(8):
            q = lax.rsqrt(a[j][j])
            r = q * q
            scale = jnp.where(sub == j, q, scale)
            w = [None] * 8
            for i in range(j + 1, 8):
                w[i] = a[i][j] * r
            for i in range(j + 1, 8):
                for m in range(j + 1, i + 1):
                    a[i][m] = a[i][m] - w[i] * a[m][j]
            unit = jnp.where(sub > j, c[j] * r, 0.0)
            for m in range(j + 1, 8):
                c[m] = c[m] - c[j] * w[m]
            pivot = jnp.broadcast_to(row[j : j + 1, :], (8, 256))
            row = row - jnp.concatenate([unit, unit], axis=1) * pivot
            if not last:
                lead = n[j] * r
                for m in range(j + 1, 8):
                    n[m] = n[m] - n[j] * w[m]
                below = below - jnp.concatenate([lead, lead], axis=1) * pivot
        done = row * jnp.concatenate([scale, scale], axis=1)
        u_ref[lo : lo + 8, :] = done
        before = done
        if not last:
            row = below


def gather_kernel(x_hbm, y_hbm, t_out, f_out, y_out, a_out, head, tile, other, hold, t_ref, s_ref, u_ref, sems, tree_recv, z_recv, h_recv, d_recv, t_recv, t_send, r_send, l_send, d_send, c_send, tree_send, root_send, z_send, pair_send, pair_recv):
    s = lax.axis_index("srow")
    z = lax.axis_index("scol")
    core = s % 2
    node = s // 2
    x = node % 4
    y = node // 4
    is_root = node == 0
    is_first = jnp.logical_and(s == 0, z == 0)

    def at(px, py, pcore, pz):
        return (((py % 4) * 4 + px % 4) * 2 + pcore, pz)

    def remote(src, dst, send, recv, device):
        return pltpu.make_async_remote_copy(src_ref=src, dst_ref=dst, send_sem=send, recv_sem=recv, device_id=device, device_id_type=MESH)

    mate = at(x, y, 1 - core, z)
    barrier = pltpu.get_barrier_semaphore()

    def greet_plane(j, carry):
        pl.semaphore_signal(barrier, inc=1, device_id=((s + j) % 32, z), device_id_type=MESH)
        return carry

    def greet_line(j, carry):
        pl.semaphore_signal(barrier, inc=1, device_id=(s, (z + j) % 8), device_id_type=MESH)
        return carry

    lax.fori_loop(1, 32, greet_plane, 0)
    lax.fori_loop(1, 8, greet_line, 0)

    @pl.when(z == 0)
    def _():
        fetch = pltpu.make_async_copy(x_hbm.at[:, 0:8, :], head, sems.at[0])
        fetch.start()
        fetch.wait()
        for q in range(4):
            tile[:, 128 * q : 128 * q + 128] = head[:, q, :]

    pieces = []
    for k in range(4):
        if k:
            pieces.append((k, 0, 128 * k))
        pieces.append((k, 128 * k, 128))

    def piece_rows(k, q):
        return pl.ds(pl.multiple_of(128 * k + 32 * q, 32), 32)

    def lanes(p, shift=0):
        return slice(pieces[p][1] + shift, pieces[p][1] + pieces[p][2] + shift)

    def feed(begin, end):
        def send(n, carry):
            for t in range(4):
                target = at(STEPS[t][0] + 4, STEPS[t][1] + 4, 1, z)

                @pl.when(n < 16)
                def _():
                    block = pl.ds(128 * t + 8 * n, 8)
                    remote(x_hbm.at[block], f_out.at[block], root_send.at[t], tree_recv.at[t, n], target).start()

                @pl.when(n >= 16)
                def _():
                    block = pl.ds(pl.multiple_of(128 * t + 16 * (n - 16), 16), 16)
                    remote(y_hbm.at[block], y_out.at[block], root_send.at[t + 4], tree_recv.at[t, n], target).start()

            return carry

        lax.fori_loop(begin, end, send, 0)

    def hand_over():
        remote(x_hbm, f_out, pair_send.at[0], pair_recv.at[0], mate).start()
        remote(y_hbm, y_out, pair_send.at[1], pair_recv.at[1], mate).start()

    def give_tile():
        remote(tile, other, sems.at[1], sems.at[2], mate).start()
        pltpu.make_async_copy(tile, a_out, sems.at[3]).start()

    @pl.when(is_first)
    def _():
        t_ref[:, 0:512] = tile[...]
        t_ref[:, 512:1024] = jnp.zeros((512, 512), F32)
        rows = lax.broadcasted_iota(jnp.int32, (128, 128), 0)
        cols = lax.broadcasted_iota(jnp.int32, (128, 128), 1)

        def give(p):
            k = pieces[p][0]
            for q, (dx, dy) in enumerate(STEPS):
                remote(t_ref.at[128 * k + 32 * q : 128 * k + 32 * q + 32, lanes(p, 512)], hold.at[k, :, lanes(p)], r_send.at[p], h_recv.at[p], at(dx + 4, dy + 4, 0, 0)).start()

        def given(p):
            part = t_ref.at[0:128, lanes(p, 512)]
            remote(part, part, r_send.at[p], h_recv.at[p], mate).wait_send()

        def step(k, carry):
            base = pl.multiple_of(k * 128, 128)
            mine = pl.ds(base, 128)
            s_ref[:, 0:128] = t_ref[mine, mine]
            s_ref[:, 128:256] = (rows == cols).astype(F32)
            factor_block(s_ref, u_ref)
            inverse = u_ref[:, 128:256]
            t_ref[mine, mine] = jnp.where(rows <= cols, u_ref[:, 0:128], 0.0)
            t_ref[mine, pl.ds(pl.multiple_of(base + 512, 128), 128)] = inverse

            @pl.when(k == 0)
            def _():
                pl.semaphore_wait(barrier, 38)

            for j in range(4):

                @pl.when(k == j)
                def _():
                    give(2 * j)
                    if j:
                        given(2 * j - 1)

            @pl.when(k == 0)
            def _():
                give_tile()
                feed(0, 13)

            @pl.when(k == 1)
            def _():
                feed(13, CHUNKS)

            @pl.when(k == 2)
            def _():
                hand_over()

            middle = pl.ds(pl.multiple_of(base + 128, 128), 384)
            t_ref[mine, middle] = jnp.dot(inverse, t_ref[mine, middle], precision=HIGHEST, preferred_element_type=F32)

            @pl.when(k < 3)
            def _():
                later = pl.multiple_of(base + 128, 128)
                coming = pl.ds(later, 128)
                window = pl.ds(later, 640)

                def take(m, inner):
                    above = pl.ds(pl.multiple_of(m * 128, 128), 128)
                    t_ref[coming, window] = t_ref[coming, window] - tdot(t_ref[above, coming], t_ref[above, window])
                    return inner

                lax.fori_loop(0, k + 1, take, 0)

            for j in range(3):

                @pl.when(k == j)
                def _():
                    give(2 * j + 1)

            return carry

        lax.fori_loop(0, 4, step, 0)
        keep = pltpu.make_async_copy(t_ref.at[:, 0:512], t_out.at[:, 0:512], sems.at[0])
        keep.start()
        for j in range(4):
            given(2 * j)
        keep.wait()

    @pl.when(jnp.logical_not(is_first))
    def _():
        pl.semaphore_wait(barrier, 38)

        @pl.when(z == 0)
        def _():
            give_tile()

        @pl.when(s == 0)
        def _():
            feed(0, CHUNKS)
            hand_over()

    quarter = jnp.where(x == 1, 0, jnp.where(y == 1, 1, jnp.where(x == 3, 2, 3)))
    holder = jnp.logical_or(jnp.logical_and(y == 0, x % 2 == 1), jnp.logical_and(x == 0, y % 2 == 1))
    on_line = core == jnp.logical_or(holder, is_root).astype(jnp.int32)

    z_depth = jnp.minimum(z, 8 - z)
    z_up = z < 4
    z_down = jnp.logical_or(z == 0, z > 5)

    def z_step(i):
        for k in range(2):

            @pl.when(i % 2 == k)
            def _():
                rows = pl.ds(pl.multiple_of(32 * (i // 2), 32), 32)
                dst = a_out if k == 0 else other

                def send(src):
                    @pl.when(z_up)
                    def _():
                        remote(src.at[rows], dst.at[rows], z_send.at[k], z_recv.at[i], (s, (z + 1) % 8)).start()

                    @pl.when(z_down)
                    def _():
                        remote(src.at[rows], dst.at[rows], z_send.at[k + 2], z_recv.at[i], (s, (z + 7) % 8)).start()

                @pl.when(z == 0)
                def _():
                    send(tile if k == 0 else other)

                @pl.when(z != 0)
                def _():
                    remote(dst.at[rows], dst.at[rows], z_send.at[k], z_recv.at[i], mate).wait_recv()
                    send(dst)
                    if k == 1:
                        remote(other.at[rows], a_out.at[rows], pair_send.at[2], pair_recv.at[2], mate).start()

    def tile_came():
        remote(tile, other, sems.at[1], sems.at[2], mate).wait_recv()

    def line_end():
        @pl.when(on_line)
        def _():
            for k in range(2):

                @pl.when(z_up)
                def _():
                    remote(a_out, a_out, z_send.at[k], pair_recv.at[2], mate).wait_send()

                @pl.when(z_down)
                def _():
                    remote(a_out, a_out, z_send.at[k + 2], pair_recv.at[2], mate).wait_send()

            @pl.when(z != 0)
            def _():
                remote(a_out, a_out, pair_send.at[2], pair_recv.at[2], mate).wait_send()

        @pl.when(jnp.logical_not(on_line))
        def _():
            @pl.when(z == 0)
            def _():
                tile_came()

            @pl.when(z != 0)
            def _():
                remote(a_out, a_out, pair_send.at[2], pair_recv.at[2], mate).wait_recv()

        @pl.when(z == 0)
        def _():
            remote(tile, other, sems.at[1], sems.at[2], mate).wait_send()
            pltpu.make_async_copy(tile, a_out, sems.at[3]).wait()

    @pl.when(core == 0)
    def _():
        @pl.when(holder)
        def _():
            for p, (k, _, _) in enumerate(pieces):
                part = hold.at[k, :, lanes(p)]
                mine = t_out.at[piece_rows(k, quarter), lanes(p, 512)]
                remote(part, part, r_send.at[p], h_recv.at[p], mate).wait_recv()

                @pl.when(z == 0)
                def _():
                    for far in (4, 3, 5, 2, 6, 1, 7):
                        remote(part, part, l_send.at[p], h_recv.at[p], (s, far)).start()

                def around(j, carry):
                    remote(part, mine, d_send.at[p], d_recv.at[p], ((s + 2 * j) % 32, z)).start()
                    return carry

                lax.fori_loop(1, 16, around, 0)
                pltpu.make_async_copy(part, mine, c_send.at[p]).start()

        @pl.when(on_line)
        def _():
            @pl.when(z == 0)
            def _():
                tile_came()

            def pass_on(i, carry):
                z_step(i)
                return carry

            lax.fori_loop(0, 32, pass_on, 0)

        for p, (k, _, _) in enumerate(pieces):

            @pl.when(holder)
            def _():
                part = t_out.at[0:96, lanes(p, 512)]
                remote(part, part, d_send.at[p], d_recv.at[p], mate).wait_recv()
                pltpu.make_async_copy(hold.at[k, :, lanes(p)], t_out.at[piece_rows(k, quarter), lanes(p, 512)], c_send.at[p]).wait()

            whole = t_out.at[128 * k : 128 * k + 128, lanes(p, 512)]

            @pl.when(jnp.logical_not(holder))
            def _():
                remote(whole, whole, d_send.at[p], d_recv.at[p], mate).wait_recv()

            remote(whole, whole, t_send.at[p], t_recv.at[p], mate).start()

        for p, (k, _, _) in enumerate(pieces):
            whole = t_out.at[128 * k : 128 * k + 128, lanes(p, 512)]
            remote(whole, whole, t_send.at[p], t_recv.at[p], mate).wait_send()

            @pl.when(holder)
            def _():
                part = t_ref.at[0:480, lanes(p)]
                remote(part, part, d_send.at[p], d_recv.at[p], mate).wait_send()

                @pl.when(z == 0)
                def _():
                    part = t_ref.at[0:224, lanes(p)]
                    remote(part, part, l_send.at[p], h_recv.at[p], mate).wait_send()

        line_end()

        @pl.when(is_root)
        def _():
            remote(f_out, f_out, pair_send.at[0], pair_recv.at[0], mate).wait_send()
            remote(y_out, y_out, pair_send.at[1], pair_recv.at[1], mate).wait_send()
            for t in range(4):
                f_part = f_out.at[0:128]
                y_part = y_out.at[0:128]
                remote(f_part, f_part, root_send.at[t], pair_recv.at[0], mate).wait_send()
                remote(y_part, y_part, root_send.at[t + 4], pair_recv.at[1], mate).wait_send()

        @pl.when(jnp.logical_not(is_root))
        def _():
            remote(f_out, f_out, pair_send.at[0], pair_recv.at[0], mate).wait_recv()
            remote(y_out, y_out, pair_send.at[1], pair_recv.at[1], mate).wait_recv()

    @pl.when(core == 1)
    def _():
        places = ((x, y), (y, 4 - x), (4 - x, 4 - y), (4 - y, x))
        starts = []
        gives = []
        for t in range(4):
            u = (places[t][1] % 4) * 4 + places[t][0] % 4
            depth = 0
            for n, d in enumerate(DEPTH):
                depth = depth + d * (u == n).astype(jnp.int32)
            starts.append(depth * HOP)
            mine = [None] * 4
            for d in range(4):
                hit = u == KIDS[d][0]
                for n in KIDS[d][1:]:
                    hit = jnp.logical_or(hit, u == n)
                mine[(d + t) % 4] = hit
            gives.append(mine)

        def f_copy(t, n, send, recv, device):
            block = f_out.at[pl.ds(128 * t + 8 * n, 8)]
            return remote(block, block, send, recv, device)

        def y_copy(t, n, send, recv, device):
            block = y_out.at[pl.ds(pl.multiple_of(128 * t + 16 * n, 16), 16)]
            return remote(block, block, send, recv, device)

        def neighbour(d):
            return at(x + STEPS[d][0] + 4, y + STEPS[d][1] + 4, 1, z)

        def flow(kind, t, n, copy):
            copy(t, n, tree_send.at[kind, 0], tree_recv.at[t, n + 16 * kind], mate).wait_recv()
            for d in range(4):

                @pl.when(gives[t][d])
                def _():
                    copy(t, n, tree_send.at[kind, 4 * t + d], tree_recv.at[t, n + 16 * kind], neighbour(d)).start()

            copy(t, n, pair_send.at[kind], pair_recv.at[kind], mate).start()

        def slot(i, carry):
            for t in range(4):
                n = jnp.where(is_root, -1, i - starts[t])

                @pl.when(jnp.logical_and(n >= 0, n < 16))
                def _():
                    flow(0, t, n, f_copy)

                @pl.when(jnp.logical_and(n >= 16, n < CHUNKS))
                def _():
                    flow(1, t, n - 16, y_copy)

            zi = jnp.where(on_line, i - HOP * z_depth - 4, -1)

            @pl.when(jnp.logical_and(z == 0, zi == 0))
            def _():
                tile_came()

            @pl.when(jnp.logical_and(zi >= 0, zi < 32))
            def _():
                z_step(zi)

            return carry

        lax.fori_loop(0, 36 + 4 * HOP, slot, 0)

        f_part = f_out.at[0:128]
        y_part = y_out.at[0:128]

        @pl.when(is_root)
        def _():
            remote(f_out, f_out, pair_send.at[0], pair_recv.at[0], mate).wait_recv()
            remote(y_out, y_out, pair_send.at[1], pair_recv.at[1], mate).wait_recv()

        @pl.when(jnp.logical_not(is_root))
        def _():
            for t in range(4):
                for d in range(4):

                    @pl.when(gives[t][d])
                    def _():
                        remote(f_part, f_part, tree_send.at[0, 4 * t + d], pair_recv.at[0], mate).wait_send()
                        remote(y_part, y_part, tree_send.at[1, 4 * t + d], pair_recv.at[1], mate).wait_send()

            remote(f_out, f_out, pair_send.at[0], pair_recv.at[0], mate).wait_send()
            remote(y_out, y_out, pair_send.at[1], pair_recv.at[1], mate).wait_send()

        line_end()

        for p, (k, _, _) in enumerate(pieces):
            whole = t_out.at[128 * k : 128 * k + 128, lanes(p, 512)]
            remote(whole, whole, t_send.at[p], t_recv.at[p], mate).wait_recv()


def gather(x, y):
    dma = pltpu.SemaphoreType.DMA
    anyspace = pl.BlockSpec(memory_space=pl.ANY)
    return pl.pallas_call(
        gather_kernel,
        out_shape=(
            jax.ShapeDtypeStruct((512, 1024), F32),
            jax.ShapeDtypeStruct((512, 16, 128), F32),
            jax.ShapeDtypeStruct((512, 1024), F32),
            jax.ShapeDtypeStruct((512, 512), F32),
        ),
        in_specs=[pl.BlockSpec(memory_space=pltpu.HBM)] * 2,
        out_specs=[anyspace] * 4,
        scratch_shapes=[
            pltpu.VMEM((512, 8, 128), F32),
            pltpu.VMEM((512, 512), F32),
            pltpu.VMEM((512, 512), F32),
            pltpu.VMEM((4, 32, 512), F32),
            pltpu.VMEM((512, 1024), F32),
            pltpu.VMEM((128, 256), F32),
            pltpu.VMEM((128, 256), F32),
            dma((4,)),
            dma((4, CHUNKS)),
            dma((32,)),
            dma((7,)),
            dma((7,)),
            dma((7,)),
            dma((7,)),
            dma((7,)),
            dma((7,)),
            dma((7,)),
            dma((7,)),
            dma((2, 16)),
            dma((8,)),
            dma((4,)),
            dma((3,)),
            dma((3,)),
        ],
        compiler_params=pltpu.CompilerParams(collective_id=0, has_side_effects=True, vmem_limit_bytes=53 << 20),
        name="gather",
    )(x, y)


def split(v):
    high = v.astype(BF16)
    return high, (v - high.astype(F32)).astype(BF16)


def dot3(a, b, dims=(((1,), (0,)), ((), ()))):
    ah, al = a
    bh, bl = b
    dot = functools.partial(lax.dot_general, dimension_numbers=dims, preferred_element_type=F32)
    return dot(ah, bh) + (dot(ah, bl) + dot(al, bh))


def update_kernel(t_hbm, f_hbm, r_hbm, a_hbm, x_hbm, y_hbm, fo_hbm, yo_hbm, t, a, f, r, x, y, fo, yo, sems):
    s = lax.axis_index("srow")
    z = lax.axis_index("scol")
    loads = [
        pltpu.make_async_copy(src, dst, sems.at[i])
        for i, (src, dst) in enumerate(((t_hbm, t), (a_hbm, a), (f_hbm, f), (x_hbm, x), (r_hbm, r), (y_hbm, y)))
    ]
    halves = (slice(0, 512), slice(512, 1024))
    stores = [pltpu.make_async_copy(fo, fo_hbm, sems.at[6])]
    stores += [pltpu.make_async_copy(yo.at[:, half], yo_hbm.at[:, half], sems.at[7 + i]) for i, half in enumerate(halves)]
    for load in loads:
        load.start()
    loads[0].wait()
    loads[1].wait()

    def lane(ref, i):
        return ref.at[pl.ds(i, 512, stride=16), :]

    def inverse_rows(k):
        rows = slice(128 * k, 128 * k + 128)
        own = t[rows, 512 + 128 * k : 640 + 128 * k]
        if k == 0:
            return own
        left = dot3(split(own), split(t[rows, 512 : 512 + 128 * k]))
        return jnp.concatenate([left, own], axis=1)

    def padded_rows(k):
        rows = inverse_rows(k)
        return rows if k == 3 else jnp.concatenate([rows, jnp.zeros((128, 384 - 128 * k), F32)], axis=1)

    @pl.when(s != 0)
    def _():
        inverse = split(jnp.concatenate([padded_rows(k) for k in range(4)], axis=0))
        panel = dot3(split(a[...]), inverse, (((1,), (1,)), ((), ())))
        q = split(dot3(split(panel), inverse))
        loads[2].wait()
        loads[3].wait()
        for c in range(4):
            right = split(jnp.concatenate([lane(f, 4 * c + j)[...] for j in range(4)], axis=1))
            change = dot3(q, right)
            for j in range(4):
                lane(fo, 4 * c + j)[...] = lane(x, 4 * c + j)[...] - change[:, 128 * j : 128 * j + 128]

        @pl.when(z == 0)
        def _():
            for j in range(4):
                lane(fo, j)[...] = panel[:, 128 * j : 128 * j + 128]

        stores[0].start()
        loads[4].wait()
        loads[5].wait()
        for c, part in enumerate(halves):
            yo[:, part] = y[:, part] - dot3(q, split(r[:, part]))
            stores[1 + c].start()

    @pl.when(s == 0)
    def _():
        fo[...] = jnp.zeros_like(fo)

        @pl.when(z == 0)
        def _():
            rows = lax.broadcasted_iota(jnp.int32, (512, 512), 0)
            cols = lax.broadcasted_iota(jnp.int32, (512, 512), 1)
            lower = jnp.where(rows >= cols, t[:, 0:512].T, 0.0)
            for j in range(4):
                lane(fo, j)[...] = lower[:, 128 * j : 128 * j + 128]

        stores[0].start()
        for load in loads[2:]:
            load.wait()
        ys = split(y[...])
        for k in range(4):
            width = 128 * k + 128
            yo[128 * k : width, :] = dot3(split(inverse_rows(k)), (ys[0][:width], ys[1][:width]))
        stores[1].start()
        stores[2].start()

    for store in stores:
        store.wait()


def update(t, f, r, a, x, y):
    anyspace = pl.BlockSpec(memory_space=pl.ANY)
    return pl.pallas_call(
        update_kernel,
        out_shape=(jax.ShapeDtypeStruct((8192, 128), F32), jax.ShapeDtypeStruct((512, 1024), F32)),
        in_specs=[anyspace] * 6,
        out_specs=[anyspace] * 2,
        scratch_shapes=[
            pltpu.VMEM((512, 1024), F32),
            pltpu.VMEM((512, 512), F32),
            pltpu.VMEM((8192, 128), F32),
            pltpu.VMEM((512, 1024), F32),
            pltpu.VMEM((8192, 128), F32),
            pltpu.VMEM((512, 1024), F32),
            pltpu.VMEM((8192, 128), F32),
            pltpu.VMEM((512, 1024), F32),
            pltpu.SemaphoreType.DMA((9,)),
        ],
        compiler_params=pltpu.CompilerParams(vmem_limit_bytes=56 << 20),
        name="update",
    )(t, f, r, a, x, y)


def per_device(factor_state, data):
    x = factor_state.reshape(512, 16, 128)
    y = data.reshape(512, 1024)
    t, f, r, a = gather(x, y)
    factor_out, data_out = update(t, f.reshape(8192, 128), r, a, x.reshape(8192, 128), y)
    return factor_out.reshape(factor_state.shape), data_out.reshape(data.shape)


def solution(mesh):
    specs = (P("srow", None, None, "scol", None), P("srow", None, "scol"))
    return jax.shard_map(per_device, mesh=mesh, in_specs=specs, out_specs=specs, check_vma=False)
```

```python
import functools

import jax
import jax.numpy as jnp
from jax import lax
from jax.experimental import pallas as pl
from jax.experimental.pallas import tpu as pltpu
from jax.sharding import PartitionSpec as P

F32 = jnp.float32
BF16 = jnp.bfloat16
HIGHEST = lax.Precision.HIGHEST
MESH = pl.DeviceIdType.MESH
STEPS = ((1, 0), (0, 1), (-1, 0), (0, -1))
DEPTH = (0, 1, 2, 3, 3, 2, 3, 4, 4, 3, 4, 5, 3, 2, 3, 4)
KIDS = ((0, 1, 2, 5, 6, 10, 14), (1, 5), (5, 9, 13), (1, 2, 14))
HOP = 4
CHUNKS = 24


def tdot(a, b):
    return lax.dot_general(a, b, (((0,), (0,)), ((), ())), precision=HIGHEST, preferred_element_type=F32)


def factor_block(s_ref, u_ref):
    sub = lax.broadcasted_iota(jnp.int32, (8, 128), 0)
    row = s_ref[0:8, :]
    before = None
    for k in range(16):
        lo = 8 * k
        last = k == 15
        if before is not None and not last:
            s_ref[lo + 8 : 128, :] = s_ref[lo + 8 : 128, :] - tdot(before[:, lo + 8 : 128], before)
        c = [jnp.broadcast_to(row[:, lo + m : lo + m + 1], (8, 128)) for m in range(8)]
        a = [[jnp.broadcast_to(c[j][i : i + 1, :], (8, 128)) if i >= j else None for j in range(8)] for i in range(8)]
        if not last:
            below = s_ref[lo + 8 : lo + 16, :]
            n = [jnp.broadcast_to(below[:, lo + m : lo + m + 1], (8, 128)) for m in range(8)]
        scale = jnp.zeros((8, 128), F32)
        for j in range(8):
            q = lax.rsqrt(a[j][j])
            r = q * q
            scale = jnp.where(sub == j, q, scale)
            w = [None] * 8
            for i in range(j + 1, 8):
                w[i] = a[i][j] * r
            for i in range(j + 1, 8):
                for m in range(j + 1, i + 1):
                    a[i][m] = a[i][m] - w[i] * a[m][j]
            unit = jnp.where(sub > j, c[j] * r, 0.0)
            for m in range(j + 1, 8):
                c[m] = c[m] - c[j] * w[m]
            pivot = jnp.broadcast_to(row[j : j + 1, :], (8, 256))
            row = row - jnp.concatenate([unit, unit], axis=1) * pivot
            if not last:
                lead = n[j] * r
                for m in range(j + 1, 8):
                    n[m] = n[m] - n[j] * w[m]
                below = below - jnp.concatenate([lead, lead], axis=1) * pivot
        done = row * jnp.concatenate([scale, scale], axis=1)
        u_ref[lo : lo + 8, :] = done
        before = done
        if not last:
            row = below


def gather_kernel(x_hbm, y_hbm, t_out, f_out, y_out, a_out, head, tile, other, hold, t_ref, s_ref, u_ref, sems, tree_recv, z_recv, h_recv, d_recv, t_recv, t_send, r_send, l_send, d_send, c_send, tree_send, root_send, z_send, pair_send, pair_recv):
    s = lax.axis_index("srow")
    z = lax.axis_index("scol")
    core = s % 2
    node = s // 2
    x = node % 4
    y = node // 4
    is_root = node == 0
    is_first = jnp.logical_and(s == 0, z == 0)

    def at(px, py, pcore, pz):
        return (((py % 4) * 4 + px % 4) * 2 + pcore, pz)

    def remote(src, dst, send, recv, device):
        return pltpu.make_async_remote_copy(src_ref=src, dst_ref=dst, send_sem=send, recv_sem=recv, device_id=device, device_id_type=MESH)

    mate = at(x, y, 1 - core, z)
    barrier = pltpu.get_barrier_semaphore()

    def greet_plane(j, carry):
        pl.semaphore_signal(barrier, inc=1, device_id=((s + j) % 32, z), device_id_type=MESH)
        return carry

    def greet_line(j, carry):
        pl.semaphore_signal(barrier, inc=1, device_id=(s, (z + j) % 8), device_id_type=MESH)
        return carry

    lax.fori_loop(1, 32, greet_plane, 0)
    lax.fori_loop(1, 8, greet_line, 0)

    @pl.when(z == 0)
    def _():
        fetch = pltpu.make_async_copy(x_hbm.at[:, 0:8, :], head, sems.at[0])
        fetch.start()
        fetch.wait()
        for q in range(4):
            tile[:, 128 * q : 128 * q + 128] = head[:, q, :]

    pieces = []
    for k in range(4):
        if k:
            pieces.append((k, 0, 128 * k))
        pieces.append((k, 128 * k, 128))

    def piece_rows(k, q):
        return pl.ds(pl.multiple_of(128 * k + 32 * q, 32), 32)

    def lanes(p, shift=0):
        return slice(pieces[p][1] + shift, pieces[p][1] + pieces[p][2] + shift)

    def feed(begin, end):
        def send(n, carry):
            for t in range(4):
                target = at(STEPS[t][0] + 4, STEPS[t][1] + 4, 1, z)

                @pl.when(n < 4)
                def _():
                    block = pl.ds(128 * t + 32 * n, 32)
                    remote(x_hbm.at[block], f_out.at[block], root_send.at[t], tree_recv.at[t, 4 * n], target).start()

                @pl.when(n >= 4)
                def _():
                    block = pl.ds(pl.multiple_of(128 * t + 64 * (n - 4), 64), 64)
                    remote(y_hbm.at[block], y_out.at[block], root_send.at[t + 4], tree_recv.at[t, 4 * n], target).start()

            return carry

        lax.fori_loop(begin, end, send, 0)

    def hand_over():
        remote(x_hbm, f_out, pair_send.at[0], pair_recv.at[0], mate).start()
        remote(y_hbm, y_out, pair_send.at[1], pair_recv.at[1], mate).start()

    def give_tile():
        remote(tile, other, sems.at[1], sems.at[2], mate).start()
        pltpu.make_async_copy(tile, a_out, sems.at[3]).start()

    @pl.when(is_first)
    def _():
        t_ref[:, 0:512] = tile[...]
        t_ref[:, 512:1024] = jnp.zeros((512, 512), F32)
        rows = lax.broadcasted_iota(jnp.int32, (128, 128), 0)
        cols = lax.broadcasted_iota(jnp.int32, (128, 128), 1)

        def give(p):
            k = pieces[p][0]
            for q, (dx, dy) in enumerate(STEPS):
                remote(t_ref.at[128 * k + 32 * q : 128 * k + 32 * q + 32, lanes(p, 512)], hold.at[k, :, lanes(p)], r_send.at[p], h_recv.at[p], at(dx + 4, dy + 4, 0, 0)).start()

        def given(p):
            part = t_ref.at[0:128, lanes(p, 512)]
            remote(part, part, r_send.at[p], h_recv.at[p], mate).wait_send()

        def step(k, carry):
            base = pl.multiple_of(k * 128, 128)
            mine = pl.ds(base, 128)
            s_ref[:, 0:128] = t_ref[mine, mine]
            s_ref[:, 128:256] = (rows == cols).astype(F32)
            factor_block(s_ref, u_ref)
            inverse = u_ref[:, 128:256]
            t_ref[mine, mine] = jnp.where(rows <= cols, u_ref[:, 0:128], 0.0)
            t_ref[mine, pl.ds(pl.multiple_of(base + 512, 128), 128)] = inverse

            @pl.when(k == 0)
            def _():
                pl.semaphore_wait(barrier, 38)

            for j in range(4):

                @pl.when(k == j)
                def _():
                    give(2 * j)
                    if j:
                        given(2 * j - 1)

            @pl.when(k == 0)
            def _():
                give_tile()
                feed(0, 2)

            @pl.when(k == 1)
            def _():
                feed(2, 4)

            @pl.when(k == 2)
            def _():
                feed(4, 6)

            @pl.when(k == 3)
            def _():
                hand_over()

            middle = pl.ds(pl.multiple_of(base + 128, 128), 384)
            t_ref[mine, middle] = jnp.dot(inverse, t_ref[mine, middle], precision=HIGHEST, preferred_element_type=F32)

            @pl.when(k < 3)
            def _():
                later = pl.multiple_of(base + 128, 128)
                coming = pl.ds(later, 128)
                window = pl.ds(later, 640)

                def take(m, inner):
                    above = pl.ds(pl.multiple_of(m * 128, 128), 128)
                    t_ref[coming, window] = t_ref[coming, window] - tdot(t_ref[above, coming], t_ref[above, window])
                    return inner

                lax.fori_loop(0, k + 1, take, 0)

            for j in range(3):

                @pl.when(k == j)
                def _():
                    give(2 * j + 1)

            return carry

        lax.fori_loop(0, 4, step, 0)
        keep = pltpu.make_async_copy(t_ref.at[:, 0:512], t_out.at[:, 0:512], sems.at[0])
        keep.start()
        for j in range(4):
            given(2 * j)
        keep.wait()

    @pl.when(jnp.logical_not(is_first))
    def _():
        pl.semaphore_wait(barrier, 38)

        @pl.when(z == 0)
        def _():
            give_tile()

        @pl.when(s == 0)
        def _():
            feed(0, 6)
            hand_over()

    quarter = jnp.where(x == 1, 0, jnp.where(y == 1, 1, jnp.where(x == 3, 2, 3)))
    holder = jnp.logical_or(jnp.logical_and(y == 0, x % 2 == 1), jnp.logical_and(x == 0, y % 2 == 1))
    on_line = core == jnp.logical_or(holder, is_root).astype(jnp.int32)

    z_depth = jnp.minimum(z, 8 - z)
    z_up = z < 4
    z_down = jnp.logical_or(z == 0, z > 5)

    def z_step(i):
        for k in range(2):

            @pl.when(i % 2 == k)
            def _():
                rows = pl.ds(pl.multiple_of(32 * (i // 2), 32), 32)
                dst = a_out if k == 0 else other

                def send(src):
                    @pl.when(z_up)
                    def _():
                        remote(src.at[rows], dst.at[rows], z_send.at[k], z_recv.at[i], (s, (z + 1) % 8)).start()

                    @pl.when(z_down)
                    def _():
                        remote(src.at[rows], dst.at[rows], z_send.at[k + 2], z_recv.at[i], (s, (z + 7) % 8)).start()

                @pl.when(z == 0)
                def _():
                    send(tile if k == 0 else other)

                @pl.when(z != 0)
                def _():
                    remote(dst.at[rows], dst.at[rows], z_send.at[k], z_recv.at[i], mate).wait_recv()
                    send(dst)
                    if k == 1:
                        remote(other.at[rows], a_out.at[rows], pair_send.at[2], pair_recv.at[2], mate).start()

    def tile_came():
        remote(tile, other, sems.at[1], sems.at[2], mate).wait_recv()

    def line_end():
        @pl.when(on_line)
        def _():
            for k in range(2):

                @pl.when(z_up)
                def _():
                    remote(a_out, a_out, z_send.at[k], pair_recv.at[2], mate).wait_send()

                @pl.when(z_down)
                def _():
                    remote(a_out, a_out, z_send.at[k + 2], pair_recv.at[2], mate).wait_send()

            @pl.when(z != 0)
            def _():
                remote(a_out, a_out, pair_send.at[2], pair_recv.at[2], mate).wait_send()

        @pl.when(jnp.logical_not(on_line))
        def _():
            @pl.when(z == 0)
            def _():
                tile_came()

            @pl.when(z != 0)
            def _():
                remote(a_out, a_out, pair_send.at[2], pair_recv.at[2], mate).wait_recv()

        @pl.when(z == 0)
        def _():
            remote(tile, other, sems.at[1], sems.at[2], mate).wait_send()
            pltpu.make_async_copy(tile, a_out, sems.at[3]).wait()

    @pl.when(core == 0)
    def _():
        @pl.when(holder)
        def _():
            for p, (k, _, _) in enumerate(pieces):
                part = hold.at[k, :, lanes(p)]
                mine = t_out.at[piece_rows(k, quarter), lanes(p, 512)]
                remote(part, part, r_send.at[p], h_recv.at[p], mate).wait_recv()

                @pl.when(z == 0)
                def _():
                    for far in (4, 3, 5, 2, 6, 1, 7):
                        remote(part, part, l_send.at[p], h_recv.at[p], (s, far)).start()

                def around(j, carry):
                    remote(part, mine, d_send.at[p], d_recv.at[p], ((s + 2 * j) % 32, z)).start()
                    return carry

                lax.fori_loop(1, 16, around, 0)
                pltpu.make_async_copy(part, mine, c_send.at[p]).start()

        @pl.when(on_line)
        def _():
            @pl.when(z == 0)
            def _():
                tile_came()

            def pass_on(i, carry):
                z_step(i)
                return carry

            lax.fori_loop(0, 32, pass_on, 0)

        for p, (k, _, _) in enumerate(pieces):

            @pl.when(holder)
            def _():
                part = t_out.at[0:96, lanes(p, 512)]
                remote(part, part, d_send.at[p], d_recv.at[p], mate).wait_recv()
                pltpu.make_async_copy(hold.at[k, :, lanes(p)], t_out.at[piece_rows(k, quarter), lanes(p, 512)], c_send.at[p]).wait()

            whole = t_out.at[128 * k : 128 * k + 128, lanes(p, 512)]

            @pl.when(jnp.logical_not(holder))
            def _():
                remote(whole, whole, d_send.at[p], d_recv.at[p], mate).wait_recv()

            remote(whole, whole, t_send.at[p], t_recv.at[p], mate).start()

        for p, (k, _, _) in enumerate(pieces):
            whole = t_out.at[128 * k : 128 * k + 128, lanes(p, 512)]
            remote(whole, whole, t_send.at[p], t_recv.at[p], mate).wait_send()

            @pl.when(holder)
            def _():
                part = t_ref.at[0:480, lanes(p)]
                remote(part, part, d_send.at[p], d_recv.at[p], mate).wait_send()

                @pl.when(z == 0)
                def _():
                    part = t_ref.at[0:224, lanes(p)]
                    remote(part, part, l_send.at[p], h_recv.at[p], mate).wait_send()

        line_end()

        @pl.when(is_root)
        def _():
            remote(f_out, f_out, pair_send.at[0], pair_recv.at[0], mate).wait_send()
            remote(y_out, y_out, pair_send.at[1], pair_recv.at[1], mate).wait_send()
            for t in range(4):
                f_part = f_out.at[0:128]
                y_part = y_out.at[0:128]
                remote(f_part, f_part, root_send.at[t], pair_recv.at[0], mate).wait_send()
                remote(y_part, y_part, root_send.at[t + 4], pair_recv.at[1], mate).wait_send()

        @pl.when(jnp.logical_not(is_root))
        def _():
            remote(f_out, f_out, pair_send.at[0], pair_recv.at[0], mate).wait_recv()
            remote(y_out, y_out, pair_send.at[1], pair_recv.at[1], mate).wait_recv()

    @pl.when(core == 1)
    def _():
        places = ((x, y), (y, 4 - x), (4 - x, 4 - y), (4 - y, x))
        starts = []
        gives = []
        for t in range(4):
            u = (places[t][1] % 4) * 4 + places[t][0] % 4
            depth = 0
            for n, d in enumerate(DEPTH):
                depth = depth + d * (u == n).astype(jnp.int32)
            starts.append(depth * HOP)
            mine = [None] * 4
            for d in range(4):
                hit = u == KIDS[d][0]
                for n in KIDS[d][1:]:
                    hit = jnp.logical_or(hit, u == n)
                mine[(d + t) % 4] = hit
            gives.append(mine)

        def f_copy(t, n, send, recv, device):
            block = f_out.at[pl.ds(128 * t + 8 * n, 8)]
            return remote(block, block, send, recv, device)

        def y_copy(t, n, send, recv, device):
            block = y_out.at[pl.ds(pl.multiple_of(128 * t + 16 * n, 16), 16)]
            return remote(block, block, send, recv, device)

        def neighbour(d):
            return at(x + STEPS[d][0] + 4, y + STEPS[d][1] + 4, 1, z)

        def flow(kind, t, n, copy):
            early = starts[t] == HOP

            @pl.when(jnp.logical_not(early))
            def _():
                copy(t, n, tree_send.at[kind, 0], tree_recv.at[t, n + 16 * kind], mate).wait_recv()

            @pl.when(jnp.logical_and(early, n % 4 == 0))
            def _():
                if kind == 0:
                    group = f_out.at[pl.ds(128 * t + 8 * n, 32)]
                else:
                    group = y_out.at[pl.ds(pl.multiple_of(128 * t + 16 * n, 16), 64)]
                remote(group, group, tree_send.at[kind, 0], tree_recv.at[t, n + 16 * kind], mate).wait_recv()

            for d in range(4):

                @pl.when(gives[t][d])
                def _():
                    copy(t, n, tree_send.at[kind, 4 * t + d], tree_recv.at[t, n + 16 * kind], neighbour(d)).start()

            copy(t, n, pair_send.at[kind], pair_recv.at[kind], mate).start()

        def slot(i, carry):
            for t in range(4):
                n = jnp.where(is_root, -1, i - starts[t])

                @pl.when(jnp.logical_and(n >= 0, n < 16))
                def _():
                    flow(0, t, n, f_copy)

                @pl.when(jnp.logical_and(n >= 16, n < CHUNKS))
                def _():
                    flow(1, t, n - 16, y_copy)

            zi = jnp.where(on_line, i - HOP * z_depth - 4, -1)

            @pl.when(jnp.logical_and(z == 0, zi == 0))
            def _():
                tile_came()

            @pl.when(jnp.logical_and(zi >= 0, zi < 32))
            def _():
                z_step(zi)

            return carry

        lax.fori_loop(0, 36 + 4 * HOP, slot, 0)

        f_part = f_out.at[0:128]
        y_part = y_out.at[0:128]

        @pl.when(is_root)
        def _():
            remote(f_out, f_out, pair_send.at[0], pair_recv.at[0], mate).wait_recv()
            remote(y_out, y_out, pair_send.at[1], pair_recv.at[1], mate).wait_recv()

        @pl.when(jnp.logical_not(is_root))
        def _():
            for t in range(4):
                for d in range(4):

                    @pl.when(gives[t][d])
                    def _():
                        remote(f_part, f_part, tree_send.at[0, 4 * t + d], pair_recv.at[0], mate).wait_send()
                        remote(y_part, y_part, tree_send.at[1, 4 * t + d], pair_recv.at[1], mate).wait_send()

            remote(f_out, f_out, pair_send.at[0], pair_recv.at[0], mate).wait_send()
            remote(y_out, y_out, pair_send.at[1], pair_recv.at[1], mate).wait_send()

        line_end()

        for p, (k, _, _) in enumerate(pieces):
            whole = t_out.at[128 * k : 128 * k + 128, lanes(p, 512)]
            remote(whole, whole, t_send.at[p], t_recv.at[p], mate).wait_recv()


def gather(x, y):
    dma = pltpu.SemaphoreType.DMA
    anyspace = pl.BlockSpec(memory_space=pl.ANY)
    return pl.pallas_call(
        gather_kernel,
        out_shape=(
            jax.ShapeDtypeStruct((512, 1024), F32),
            jax.ShapeDtypeStruct((512, 16, 128), F32),
            jax.ShapeDtypeStruct((512, 1024), F32),
            jax.ShapeDtypeStruct((512, 512), F32),
        ),
        in_specs=[pl.BlockSpec(memory_space=pltpu.HBM)] * 2,
        out_specs=[anyspace] * 4,
        scratch_shapes=[
            pltpu.VMEM((512, 8, 128), F32),
            pltpu.VMEM((512, 512), F32),
            pltpu.VMEM((512, 512), F32),
            pltpu.VMEM((4, 32, 512), F32),
            pltpu.VMEM((512, 1024), F32),
            pltpu.VMEM((128, 256), F32),
            pltpu.VMEM((128, 256), F32),
            dma((4,)),
            dma((4, CHUNKS)),
            dma((32,)),
            dma((7,)),
            dma((7,)),
            dma((7,)),
            dma((7,)),
            dma((7,)),
            dma((7,)),
            dma((7,)),
            dma((7,)),
            dma((2, 16)),
            dma((8,)),
            dma((4,)),
            dma((3,)),
            dma((3,)),
        ],
        compiler_params=pltpu.CompilerParams(collective_id=0, has_side_effects=True, vmem_limit_bytes=53 << 20),
        name="gather",
    )(x, y)


def split(v):
    high = v.astype(BF16)
    return high, (v - high.astype(F32)).astype(BF16)


def dot3(a, b, dims=(((1,), (0,)), ((), ()))):
    ah, al = a
    bh, bl = b
    dot = functools.partial(lax.dot_general, dimension_numbers=dims, preferred_element_type=F32)
    return dot(ah, bh) + (dot(ah, bl) + dot(al, bh))


def update_kernel(t_hbm, f_hbm, r_hbm, a_hbm, x_hbm, y_hbm, fo_hbm, yo_hbm, t, a, f, r, x, y, fo, yo, sems):
    s = lax.axis_index("srow")
    z = lax.axis_index("scol")
    loads = [
        pltpu.make_async_copy(src, dst, sems.at[i])
        for i, (src, dst) in enumerate(((t_hbm, t), (a_hbm, a), (f_hbm, f), (x_hbm, x), (r_hbm, r), (y_hbm, y)))
    ]
    halves = (slice(0, 512), slice(512, 1024))
    stores = [pltpu.make_async_copy(fo, fo_hbm, sems.at[6])]
    stores += [pltpu.make_async_copy(yo.at[:, half], yo_hbm.at[:, half], sems.at[7 + i]) for i, half in enumerate(halves)]
    for load in loads:
        load.start()
    loads[0].wait()
    loads[1].wait()

    def lane(ref, i):
        return ref.at[pl.ds(i, 512, stride=16), :]

    def inverse_rows(k):
        rows = slice(128 * k, 128 * k + 128)
        own = t[rows, 512 + 128 * k : 640 + 128 * k]
        if k == 0:
            return own
        left = dot3(split(own), split(t[rows, 512 : 512 + 128 * k]))
        return jnp.concatenate([left, own], axis=1)

    def padded_rows(k):
        rows = inverse_rows(k)
        return rows if k == 3 else jnp.concatenate([rows, jnp.zeros((128, 384 - 128 * k), F32)], axis=1)

    @pl.when(s != 0)
    def _():
        inverse = split(jnp.concatenate([padded_rows(k) for k in range(4)], axis=0))
        panel = dot3(split(a[...]), inverse, (((1,), (1,)), ((), ())))
        q = split(dot3(split(panel), inverse))
        loads[2].wait()
        loads[3].wait()
        for c in range(4):
            right = split(jnp.concatenate([lane(f, 4 * c + j)[...] for j in range(4)], axis=1))
            change = dot3(q, right)
            for j in range(4):
                lane(fo, 4 * c + j)[...] = lane(x, 4 * c + j)[...] - change[:, 128 * j : 128 * j + 128]

        @pl.when(z == 0)
        def _():
            for j in range(4):
                lane(fo, j)[...] = panel[:, 128 * j : 128 * j + 128]

        stores[0].start()
        loads[4].wait()
        loads[5].wait()
        for c, part in enumerate(halves):
            yo[:, part] = y[:, part] - dot3(q, split(r[:, part]))
            stores[1 + c].start()

    @pl.when(s == 0)
    def _():
        fo[...] = jnp.zeros_like(fo)

        @pl.when(z == 0)
        def _():
            rows = lax.broadcasted_iota(jnp.int32, (512, 512), 0)
            cols = lax.broadcasted_iota(jnp.int32, (512, 512), 1)
            lower = jnp.where(rows >= cols, t[:, 0:512].T, 0.0)
            for j in range(4):
                lane(fo, j)[...] = lower[:, 128 * j : 128 * j + 128]

        stores[0].start()
        for load in loads[2:]:
            load.wait()
        ys = split(y[...])
        for k in range(4):
            width = 128 * k + 128
            yo[128 * k : width, :] = dot3(split(inverse_rows(k)), (ys[0][:width], ys[1][:width]))
        stores[1].start()
        stores[2].start()

    for store in stores:
        store.wait()


def update(t, f, r, a, x, y):
    anyspace = pl.BlockSpec(memory_space=pl.ANY)
    return pl.pallas_call(
        update_kernel,
        out_shape=(jax.ShapeDtypeStruct((8192, 128), F32), jax.ShapeDtypeStruct((512, 1024), F32)),
        in_specs=[anyspace] * 6,
        out_specs=[anyspace] * 2,
        scratch_shapes=[
            pltpu.VMEM((512, 1024), F32),
            pltpu.VMEM((512, 512), F32),
            pltpu.VMEM((8192, 128), F32),
            pltpu.VMEM((512, 1024), F32),
            pltpu.VMEM((8192, 128), F32),
            pltpu.VMEM((512, 1024), F32),
            pltpu.VMEM((8192, 128), F32),
            pltpu.VMEM((512, 1024), F32),
            pltpu.SemaphoreType.DMA((9,)),
        ],
        compiler_params=pltpu.CompilerParams(vmem_limit_bytes=56 << 20),
        name="update",
    )(t, f, r, a, x, y)


def per_device(factor_state, data):
    x = factor_state.reshape(512, 16, 128)
    y = data.reshape(512, 1024)
    t, f, r, a = gather(x, y)
    factor_out, data_out = update(t, f.reshape(8192, 128), r, a, x.reshape(8192, 128), y)
    return factor_out.reshape(factor_state.shape), data_out.reshape(data.shape)


def solution(mesh):
    specs = (P("srow", None, None, "scol", None), P("srow", None, "scol"))
    return jax.shard_map(per_device, mesh=mesh, in_specs=specs, out_specs=specs, check_vma=False)
```
